32 devices in a mesh: chain: 4 (over y, x), op: 8 (over z, core).
Axes of the slice: x: 2, y: 2, z: 4, core: 2. Of those that a mesh axis runs over, the one named last changes fastest.
Arguments:
- env_in: bfloat16 [16, 16, 128, 128], P('op'), may hold values from -6 to 6
- mps: bfloat16 [4, 4, 16, 128, 128], P('chain'), may hold values from -0.5 to 0.5
- proj: bfloat16 [4, 4, 16, 128, 128], P('chain'), may hold values from -0.5 to 0.5
- mpo: bfloat16 [4, 16, 4, 16, 4], P('chain'), may hold values from -2 to 2
- mpo_charge: int32 [16, 2], replicated, may hold values from -1 to 1
- block_sizes: int32 [5, 16], replicated, may hold values from 32 to 128
Outputs:
- env_out: bfloat16 [4, 16, 16, 128, 128], P('chain', 'op')
The draws below stay inside these ranges and needn't reach their ends.
All inputs are finite; a program needn't handle non-finite values.
Results may differ from the reference program's by a relative error of at most 0.025.
Values may be sent and summed in bfloat16 or wider, within the bound.
No kernel may reach another device: no remote copies, remote signals or barrier semaphores. Data moves between devices by JAX's collectives and lax.ppermute only.
A program may use at most 64 MiB of HBM per device.

```python
import jax
import jax.numpy as jnp
from jax import lax

MPO_BOND = 16
BLOCK_DIM = 128
UP_VALUES = 8
DOWN_VALUES = 2
SECTORS = 16
CHAIN_SITES = 4


def touch_ends(values, key, least, high):
    spot = [jax.random.randint(jax.random.fold_in(key, axis), (), 0, length) for axis, length in enumerate(values.shape)]
    widest = values.shape.index(max(values.shape))
    beside = spot[:widest] + [(spot[widest] + 1) % values.shape[widest]] + spot[widest + 1:]
    return values.at[tuple(spot)].set(least).at[tuple(beside)].set(high)


def block_scale(stream_key, extent, split, low, high):
    level, own = 1.0, jax.random.fold_in(stream_key, 6)
    for position, blocks in split:
        draws = jnp.exp(jax.random.uniform(jax.random.fold_in(own, position), (blocks,), jnp.float32, low / len(split), high / len(split)))
        level = level * jnp.repeat(draws, extent[position] // blocks).reshape([-1 if axis == position else 1 for axis in range(len(extent))])
    return level


def noise(key, dims, deviation, most, split=(), held_as=jnp.bfloat16):
    values = deviation * jax.random.normal(key, dims, jnp.float32)
    if split:
        values = values * block_scale(key, dims, split, -0.22, 0.18)
    return jnp.clip(values, -most, most).astype(held_as)


def setup_inputs(seed: int = 0) -> dict:
    seeds = jax.random.split(jax.random.key(seed), 7)
    env_in = noise(seeds[0], (MPO_BOND, SECTORS, BLOCK_DIM, BLOCK_DIM), 1.0, 6.0, ((0, 8),))
    mps = noise(seeds[1], (CHAIN_SITES, 4, SECTORS, BLOCK_DIM, BLOCK_DIM), BLOCK_DIM ** -0.5, 0.5, ((0, 4),))
    proj = noise(seeds[2], (CHAIN_SITES, 4, SECTORS, BLOCK_DIM, BLOCK_DIM), BLOCK_DIM ** -0.5, 0.5, ((0, 4),))
    mpo = noise(seeds[3], (CHAIN_SITES, MPO_BOND, 4, MPO_BOND, 4), (MPO_BOND // 2) ** -0.5, 2.0, ((0, 4),))
    mpo_charge = touch_ends(jax.random.randint(seeds[4], (MPO_BOND, 2), -1, 2), jax.random.fold_in(seeds[4], 1), -1, 1).astype(jnp.int32)
    block_sizes = touch_ends(jax.random.randint(seeds[5], (CHAIN_SITES + 1, SECTORS), BLOCK_DIM // 4, BLOCK_DIM + 1), jax.random.fold_in(seeds[5], 1), BLOCK_DIM // 4, BLOCK_DIM).astype(jnp.int32)
    return {"env_in": env_in, "mps": mps, "proj": proj, "mpo": mpo, "mpo_charge": mpo_charge, "block_sizes": block_sizes}


UP_CHARGE = (0, 1, 0, 1)
DOWN_CHARGE = (0, 0, 1, 1)


def mask_site(site_mps, site_proj, left_sizes, right_sizes):
    positions = jnp.arange(BLOCK_DIM, dtype=jnp.int32)
    up_index = jnp.arange(UP_VALUES, dtype=jnp.int32)[:, None]
    down_index = jnp.arange(DOWN_VALUES, dtype=jnp.int32)[None, :]
    left_grid = left_sizes.reshape(UP_VALUES, DOWN_VALUES)
    right_grid = jnp.pad(right_sizes.reshape(UP_VALUES, DOWN_VALUES), ((0, 1), (0, 1)))
    mps_grid = site_mps.reshape(4, UP_VALUES, DOWN_VALUES, BLOCK_DIM, BLOCK_DIM)
    proj_grid = site_proj.reshape(4, UP_VALUES, DOWN_VALUES, BLOCK_DIM, BLOCK_DIM)
    mps_parts = []
    proj_parts = []
    for phys_state in range(4):
        up_shift = UP_CHARGE[phys_state]
        down_shift = DOWN_CHARGE[phys_state]
        right_here = right_grid[up_shift:up_shift + UP_VALUES, down_shift:down_shift + DOWN_VALUES]
        row_keep = positions[None, None, :] < left_grid[:, :, None]
        column_keep = positions[None, None, :] < right_here[:, :, None]
        keep_mask = row_keep[:, :, :, None] & column_keep[:, :, None, :]
        mps_parts.append(jnp.where(keep_mask, mps_grid[phys_state], jnp.zeros_like(mps_grid[phys_state])))
        inside = (up_index + up_shift < UP_VALUES) & (down_index + down_shift < DOWN_VALUES)
        proj_parts.append(jnp.where(inside[:, :, None, None], proj_grid[phys_state], jnp.zeros_like(proj_grid[phys_state])))
    return jnp.stack(mps_parts, axis=0), jnp.stack(proj_parts, axis=0)


def mask_mpo(site_mpo, mpo_charge):
    up_state = jnp.array(UP_CHARGE, dtype=jnp.int32)
    down_state = jnp.array(DOWN_CHARGE, dtype=jnp.int32)
    up_bond = mpo_charge[:, 0]
    down_bond = mpo_charge[:, 1]
    match_up = (up_bond[:, None, None, None] + up_state[None, None, None, :]) == (up_state[None, :, None, None] + up_bond[None, None, :, None])
    match_down = (down_bond[:, None, None, None] + down_state[None, None, None, :]) == (down_state[None, :, None, None] + down_bond[None, None, :, None])
    return jnp.where(match_up & match_down, site_mpo, jnp.zeros_like(site_mpo))


def site_step(environment, mps_grid, proj_padded, mpo_masked, mpo_charge):
    env_pad = jnp.pad(environment, ((0, 0), (1, 0), (1, 0), (0, 0), (0, 0)))
    mps_pad = jnp.pad(mps_grid, ((0, 0), (1, 0), (1, 0), (0, 0), (0, 0)))
    pieces = []
    for phys_state in range(4):
        up_shift = UP_CHARGE[phys_state]
        down_shift = DOWN_CHARGE[phys_state]
        env_part = env_pad[:, 1 - up_shift:1 - up_shift + UP_VALUES, 1 - down_shift:1 - down_shift + DOWN_VALUES]
        mps_part = mps_pad[phys_state, 1 - up_shift:1 - up_shift + UP_VALUES, 1 - down_shift:1 - down_shift + DOWN_VALUES]
        product = jnp.einsum('wudab,udbc->wudac', env_part.astype(jnp.float32), mps_part.astype(jnp.float32))
        pieces.append(product.astype(jnp.bfloat16))
    mixed_rows = jnp.stack(pieces, axis=1)

    def one_bond(running, inputs):
        mixed_bond, charge_bond, mpo_bond = inputs
        term_list = []
        zero_index = jnp.zeros((), jnp.int32)
        for phys_state in range(4):
            start_up = (2 - UP_CHARGE[phys_state] + charge_bond[0]).astype(jnp.int32)
            start_down = (2 - DOWN_CHARGE[phys_state] + charge_bond[1]).astype(jnp.int32)
            chosen = lax.dynamic_slice(proj_padded, (zero_index, start_up, start_down, zero_index, zero_index), (4, UP_VALUES, DOWN_VALUES, BLOCK_DIM, BLOCK_DIM))
            one_term = jnp.einsum('tudij,udik->tudjk', chosen.astype(jnp.float32), mixed_bond[phys_state].astype(jnp.float32))
            term_list.append(one_term.astype(jnp.bfloat16))
        projected = jnp.stack(term_list, axis=0).astype(jnp.float32)
        running = running + jnp.einsum('svt,stydjk->vydjk', mpo_bond.astype(jnp.float32), projected)
        return running, None

    start_sum = jnp.zeros((MPO_BOND, UP_VALUES, DOWN_VALUES, BLOCK_DIM, BLOCK_DIM), jnp.float32)
    running, unused = lax.scan(one_bond, start_sum, (mixed_rows, mpo_charge, mpo_masked))
    return running.astype(jnp.bfloat16)


def reference(env_in, mps, proj, mpo, mpo_charge, block_sizes):
    environment = env_in.reshape(MPO_BOND, UP_VALUES, DOWN_VALUES, BLOCK_DIM, BLOCK_DIM)
    outputs = []
    for site_index in range(CHAIN_SITES):
        mps_grid, proj_grid = mask_site(mps[site_index], proj[site_index], block_sizes[site_index], block_sizes[site_index + 1])
        proj_padded = jnp.pad(proj_grid, ((0, 0), (2, 2), (2, 2), (0, 0), (0, 0)))
        mpo_masked = mask_mpo(mpo[site_index], mpo_charge)
        environment = site_step(environment, mps_grid, proj_padded, mpo_masked, mpo_charge)
        outputs.append(environment.reshape(MPO_BOND, SECTORS, BLOCK_DIM, BLOCK_DIM))
    return jnp.stack(outputs, axis=0)
```

```python
import functools

import jax
import jax.numpy as jnp
from jax import lax
from jax.experimental import pallas as pl
from jax.experimental.pallas import tpu as pltpu
from jax.sharding import PartitionSpec as P

UP_VALUES = 8
DOWN_VALUES = 2
PHYS = 4

UP_CHARGE = (0, 1, 0, 1)
DOWN_CHARGE = (0, 0, 1, 1)

MPS_BLOCKS = ((0, 0, 0), (2, 0, 0), (0, 0, 1), (1, -1, 0), (3, -1, 0), (1, -1, 1))
ROW_SHIFTS = 3
PROJ_PARTS = ((0, -1, 2), (1, -2, 2), (2, -1, 1), (3, -2, 1))
PROJ_BLOCKS = ROW_SHIFTS * sum(part[2] for part in PROJ_PARTS)


def ring_chain(position):
    return position ^ (position >> 1)


def proj_block(phys_state, shift, down):
    start = 0
    for part_state, _, downs in PROJ_PARTS:
        if part_state == phys_state:
            return start + shift * downs + down
        start += ROW_SHIFTS * downs
    return None


def masked_mpo_matrix(site_mpo, mpo_charge):
    up_state = jnp.array(UP_CHARGE, dtype=jnp.int32)
    down_state = jnp.array(DOWN_CHARGE, dtype=jnp.int32)
    up_bond = mpo_charge[:, 0]
    down_bond = mpo_charge[:, 1]
    match_up = (
        up_bond[:, None, None, None] + up_state[None, None, None, :]
        == up_state[None, :, None, None] + up_bond[None, None, :, None]
    )
    match_down = (
        down_bond[:, None, None, None] + down_state[None, None, None, :]
        == down_state[None, :, None, None] + down_bond[None, None, :, None]
    )
    masked = jnp.where(match_up & match_down, site_mpo, jnp.zeros_like(site_mpo))
    bond = site_mpo.shape[0]
    return jnp.transpose(masked, (2, 3, 1, 0)).reshape(bond * PHYS, PHYS * bond)


def site_kernel(
    site, bond, block, slots, chunks, scalars, charges, sizes, *refs
):
    refs = list(refs)
    weight_refs = [refs.pop(0) for _ in range(slots)]
    env_refs = [refs.pop(0) for _ in range(chunks)]
    out_ref, keep_ref = refs.pop(0), refs.pop(0)
    weights, mixed, summed, kron, turned, sem = refs
    row = scalars[0]
    chain_pos = scalars[1]
    op_pos = scalars[2]
    first_keep = scalars[3]

    slot = jnp.bitwise_xor(chain_pos, site)
    for index in range(slots):
        @pl.when(slot == index)
        def _():
            copy = pltpu.make_async_copy(weight_refs[index], weights, sem)
            copy.start()
            copy.wait()

    def rows_of(index):
        return weights[index * block : (index + 1) * block, :]

    row_at = lax.broadcasted_iota(jnp.int32, (block, block), 0)
    column_at = lax.broadcasted_iota(jnp.int32, (block, block), 1)
    mps_blocks = []
    for index, (phys_state, offset, down) in enumerate(MPS_BLOCKS):
        source = jnp.maximum(row + offset, 0) * DOWN_VALUES + down
        target = row * DOWN_VALUES + down + DOWN_CHARGE[phys_state]
        keep = (row_at < sizes[site, source]) & (column_at < sizes[site + 1, target])
        value = rows_of(index)
        mps_blocks.append(jnp.where(keep, value, jnp.zeros_like(value)))

    turned[...] = jnp.zeros_like(turned)
    first_proj = len(MPS_BLOCKS)
    for shift in range(ROW_SHIFTS):
        for phys_state in range(PHYS):
            for target in range(DOWN_VALUES):
                down = target - DOWN_CHARGE[phys_state]
                if down < 0:
                    continue
                value = rows_of(first_proj + proj_block(phys_state, shift, down))
                turned[
                    shift * DOWN_VALUES + target,
                    :,
                    phys_state * block : (phys_state + 1) * block,
                ] = value.T

    pairs = bond * PHYS
    wide = pairs * 8
    first_mpo = (first_proj + PROJ_BLOCKS) * block
    matrix = weights[first_mpo : first_mpo + pairs, :]
    lanes = matrix.shape[1]
    tall = (
        lax.broadcasted_iota(jnp.int32, (wide, pairs), 0) // 8
        == lax.broadcasted_iota(jnp.int32, (wide, pairs), 1)
    ).astype(jnp.bfloat16)
    across = (
        lax.broadcasted_iota(jnp.int32, (lanes, wide), 0)
        == lax.broadcasted_iota(jnp.int32, (lanes, wide), 1) // 8
    ).astype(jnp.bfloat16)
    spread = jnp.dot(tall, matrix, preferred_element_type=jnp.float32).astype(jnp.bfloat16)
    spread = jnp.dot(spread, across, preferred_element_type=jnp.float32)
    same = (
        lax.broadcasted_iota(jnp.int32, (wide, wide), 0) % 8
        == lax.broadcasted_iota(jnp.int32, (wide, wide), 1) % 8
    )
    kron[...] = jnp.where(same, spread, 0.0).astype(jnp.bfloat16)

    per_chunk = bond // chunks

    def own_rows(down):
        for index in range(chunks):
            if chunks == 2:
                yield 0, bond, env_refs[0][:, down]
                return
            first = jnp.bitwise_xor(op_pos, index) * per_chunk
            yield first, per_chunk, env_refs[index][:, 1, down]

    def prev_rows(down):
        for index in range(chunks):
            if chunks == 2:
                yield 0, bond, env_refs[1][:, down]
                return
            first = jnp.bitwise_xor(op_pos, index) * per_chunk
            yield first, per_chunk, env_refs[index][:, 0, down]

    def multiply(pieces, right, states):
        for first, count, rows in pieces:
            product = jnp.dot(
                rows.reshape(count * block, block), right, preferred_element_type=jnp.float32
            )
            for index, phys_state in enumerate(states):
                mixed[pl.ds(phys_state * bond + first, count)] = product[
                    :, index * block : (index + 1) * block
                ].reshape(count, block, block)

    for down in range(DOWN_VALUES):
        if down == 0:
            multiply(own_rows(0), mps_blocks[0], (0,))
            multiply(prev_rows(0), mps_blocks[3], (1,))
            used = 2 * bond
        else:
            multiply(own_rows(0), mps_blocks[1], (2,))
            multiply(prev_rows(0), mps_blocks[4], (3,))
            multiply(own_rows(1), mps_blocks[2], (0,))
            multiply(prev_rows(1), mps_blocks[5], (1,))
            used = 4 * bond

        def contract(index, carry):
            at = pl.multiple_of(index * 16, 16)
            low = mixed[:used, pl.ds(at, 8), :].reshape(used * 8, block)
            high = mixed[:used, pl.ds(at + 8, 8), :].reshape(used * 8, block)
            right = jnp.concatenate([low, high], axis=1).astype(jnp.bfloat16)
            got = jnp.dot(kron[:, : used * 8], right, preferred_element_type=jnp.float32)
            summed[:, pl.ds(at, 8), :] = got[:, :block].reshape(pairs, 8, block)
            summed[:, pl.ds(at + 8, 8), :] = got[:, block:].reshape(pairs, 8, block)
            return carry

        lax.fori_loop(0, block // 16, contract, 0)

        for bond_index in range(bond):
            up = charges[bond_index, 0]
            target = down + charges[bond_index, 1]
            inside = (
                (row + up >= 0)
                & (row + up < UP_VALUES)
                & (target >= 0)
                & (target < DOWN_VALUES)
            )
            entry = jnp.where(
                inside, (up + 1) * DOWN_VALUES + target, ROW_SHIFTS * DOWN_VALUES
            )
            right = (
                summed[bond_index * PHYS : (bond_index + 1) * PHYS]
                .reshape(PHYS * block, block)
                .astype(jnp.bfloat16)
            )
            value = jnp.dot(turned[entry], right, preferred_element_type=jnp.float32)
            out_ref[bond_index, down] = value.astype(jnp.bfloat16)
    keep_ref[...] = out_ref[pl.ds(first_keep, keep_ref.shape[0])]


def run_site(site, scalars, charges, sizes, weights, env, keep):
    bond = charges.shape[0]
    block = env[0].shape[-1]
    chunks = len(env)
    pairs = bond * PHYS
    vmem = pl.BlockSpec(memory_space=pltpu.VMEM)
    smem = pl.BlockSpec(memory_space=pltpu.SMEM)
    anywhere = pl.BlockSpec(memory_space=pl.ANY)
    return pl.pallas_call(
        functools.partial(site_kernel, site, bond, block, len(weights), chunks),
        out_shape=(
            jax.ShapeDtypeStruct((bond, DOWN_VALUES, block, block), jnp.bfloat16),
            jax.ShapeDtypeStruct((keep, DOWN_VALUES, block, block), jnp.bfloat16),
        ),
        in_specs=[smem] * 3 + [anywhere] * len(weights) + [vmem] * chunks,
        out_specs=(vmem, vmem),
        scratch_shapes=[
            pltpu.VMEM(weights[0].shape, jnp.bfloat16),
            pltpu.VMEM((pairs, block, block), jnp.float32),
            pltpu.VMEM((pairs, block, block), jnp.float32),
            pltpu.VMEM((pairs * 8, pairs * 8), jnp.bfloat16),
            pltpu.VMEM((ROW_SHIFTS * DOWN_VALUES + 1, block, PHYS * block), jnp.bfloat16),
            pltpu.SemaphoreType.DMA,
        ],
        compiler_params=pltpu.CompilerParams(vmem_limit_bytes=48 << 20),
        cost_estimate=pl.CostEstimate(
            flops=4 * 10**9, bytes_accessed=4 * 10**6, transcendentals=0
        ),
        name="site",
    )(scalars, charges, sizes, *weights, *env)


def gather_kernel(places, *refs):
    out_ref = refs[-1]
    for index, ref in enumerate(refs[:-1]):
        out_ref[0, :, pl.ds(places[index] * DOWN_VALUES, DOWN_VALUES)] = ref[...]


def on_device(env_in, mps, proj, mpo, mpo_charge, block_sizes):
    chain_count = lax.axis_size("chain")
    op_count = lax.axis_size("op")
    chain_pos = lax.axis_index("chain")
    op_pos = lax.axis_index("op")
    local_bond, _, block, _ = env_in.shape
    sites = block_sizes.shape[0] - 1
    spread = UP_VALUES // chain_count
    places = [0] * chain_count
    for position in range(chain_count):
        places[ring_chain(position)] = position
    place_of = jnp.array(places, dtype=jnp.int32)
    side = lax.rem(op_pos, spread)
    layer = op_pos // spread
    row = place_of[chain_pos] * spread + side

    def flat(chain, op):
        return chain * op_count + op

    both = ("chain", "op")
    everyone = [(c, o) for c in range(chain_count) for o in range(op_count)]

    mps_grid = mps[0].reshape(PHYS, UP_VALUES, DOWN_VALUES, block, block)
    proj_grid = jnp.pad(
        proj[0].reshape(PHYS, UP_VALUES, DOWN_VALUES, block, block),
        ((0, 0), (2, 1), (0, 0), (0, 0), (0, 0)),
    )
    matrix = masked_mpo_matrix(mpo[0], mpo_charge)
    matrix = jnp.pad(matrix, ((0, 0), (0, block - matrix.shape[1])))

    def weights_for(target_row):
        pieces = []
        for phys_state, offset, down in MPS_BLOCKS:
            at = jnp.maximum(target_row + offset, 0)
            pieces.append(
                lax.dynamic_slice(
                    mps_grid, (phys_state, at, down, 0, 0), (1, 1, 1, block, block)
                ).reshape(block, block)
            )
        for phys_state, offset, downs in PROJ_PARTS:
            pieces.append(
                lax.dynamic_slice(
                    proj_grid,
                    (phys_state, target_row + offset + 2, 0, 0, 0),
                    (1, ROW_SHIFTS, downs, block, block),
                ).reshape(ROW_SHIFTS * downs * block, block)
            )
        pieces.append(matrix)
        return jnp.concatenate(pieces, axis=0)

    env_grid = jnp.pad(
        env_in.reshape(local_bond, UP_VALUES, DOWN_VALUES, block, block),
        ((0, 0), (1, 0), (0, 0), (0, 0), (0, 0)),
    )

    def env_for(target_row):
        return lax.dynamic_slice_in_dim(env_grid, target_row, 2, axis=1)

    env = []
    for hop in range(op_count):
        target = jnp.bitwise_xor(op_pos, hop)
        piece = env_for(place_of[chain_pos] * spread + lax.rem(target, spread))
        if hop:
            piece = lax.ppermute(piece, "op", [(o, o ^ hop) for o in range(op_count)])
        env.append(piece)
    weights = []
    for hop in range(chain_count):
        piece = weights_for(place_of[jnp.bitwise_xor(chain_pos, hop)] * spread + side)
        if hop:
            piece = lax.ppermute(piece, "chain", [(c, c ^ hop) for c in range(chain_count)])
        weights.append(piece)

    keep = local_bond * spread
    scalars = jnp.stack([row, chain_pos, op_pos, layer * keep]).astype(jnp.int32)

    halo = []
    for c, o in everyone:
        if o % spread < spread - 1:
            halo.append((flat(c, o), flat(c, o + 1)))
        elif places[c] < chain_count - 1:
            halo.append((flat(c, o), flat(ring_chain(places[c] + 1), o - spread + 1)))

    kept = []
    for site in range(sites):
        finished, kept_part = run_site(
            site, scalars, mpo_charge, block_sizes, weights, env, keep
        )
        kept.append(kept_part)
        if site < sites - 1:
            env = [finished, lax.ppermute(finished, both, halo)]

    kept = jnp.stack(kept).reshape(
        sites, spread, local_bond, DOWN_VALUES, block, block
    )
    arrived = []
    from_rows = []
    for hop in range(chain_count):
        for turn in range(spread):
            target_chain = jnp.bitwise_xor(chain_pos, hop)
            target_side = jnp.bitwise_xor(side, turn)
            piece = lax.dynamic_slice(
                kept,
                (target_chain, target_side, 0, 0, 0, 0),
                (1, 1, local_bond, DOWN_VALUES, block, block),
            )[0, 0]
            if hop or turn:
                piece = lax.ppermute(
                    piece, both, [(flat(c, o), flat(c ^ hop, o ^ turn)) for c, o in everyone]
                )
            arrived.append(piece)
            from_rows.append(place_of[target_chain] * spread + target_side)
    vmem = pl.BlockSpec(memory_space=pltpu.VMEM)
    return pl.pallas_call(
        gather_kernel,
        out_shape=jax.ShapeDtypeStruct((1,) + env_in.shape, jnp.bfloat16),
        in_specs=[pl.BlockSpec(memory_space=pltpu.SMEM)] + [vmem] * len(arrived),
        out_specs=vmem,
        name="gather",
    )(jnp.stack(from_rows).astype(jnp.int32), *arrived)


def solution(mesh):
    return jax.shard_map(
        on_device,
        mesh=mesh,
        in_specs=(
            P("op", None, None, None),
            P("chain", None, None, None, None),
            P("chain", None, None, None, None),
            P("chain", None, None, None, None),
            P(),
            P(),
        ),
        out_specs=P("chain", "op", None, None, None),
        check_vma=False,
    )
```

```python
import functools

import jax
import jax.numpy as jnp
from jax import lax
from jax.experimental import pallas as pl
from jax.experimental.pallas import tpu as pltpu
from jax.sharding import PartitionSpec as P


UP_VALUES = 8
DOWN_VALUES = 2
PHYS = 4

UP_CHARGE = (0, 1, 0, 1)
DOWN_CHARGE = (0, 0, 1, 1)

STATE_ORDER = (0, 2, 1, 3)
MPS_PARTS = ((0, 0, 2), (2, 0, 1), (1, -1, 2), (3, -1, 1))
MPS_BLOCKS = ((0, 0, 0), (0, 0, 1), (2, 0, 0), (1, -1, 0), (1, -1, 1), (3, -1, 0))
ROW_SHIFTS = 3
PROJ_PARTS = ((0, -1, 2), (1, -2, 2), (2, -1, 1), (3, -2, 1))
GROUP = 8


VMEM = pl.BlockSpec(memory_space=pltpu.VMEM)
SMEM = pl.BlockSpec(memory_space=pltpu.SMEM)
ANY = pl.BlockSpec(memory_space=pl.ANY)
HBM = pl.BlockSpec(memory_space=pltpu.HBM)


def ring_chain(position, count):
    turned = (position + count - 1) % count
    return turned ^ (turned >> 1)


def place(chain, count):
    plain = chain ^ (chain >> 1) ^ (chain >> 2)
    return (plain + 1) % count if isinstance(chain, int) else lax.rem(plain + 1, count)


def my_row(chain_count, spread):
    side = lax.rem(lax.axis_index("op"), spread)
    return place(lax.axis_index("chain"), chain_count) * spread + side


def held_rows(spread):
    return -(-(ROW_SHIFTS + spread - 1) // spread)


def held_base(first_row, offset, holder, spread):
    rows = held_rows(spread)
    return jnp.clip(first_row + offset + holder * rows, 0, UP_VALUES - rows)


def proj_start(phys_state, spread):
    start = len(MPS_BLOCKS)
    for part_state, _, downs in PROJ_PARTS:
        if part_state == phys_state:
            return start
        start += held_rows(spread) * downs
    return start


def mpo_matrix(site_mpo):
    bond = site_mpo.shape[0]
    ordered = jnp.stack([site_mpo[:, state] for state in STATE_ORDER], axis=1)
    return jnp.transpose(ordered, (2, 3, 1, 0)).reshape(bond * PHYS, PHYS * bond)


def call(kernel, *args, **options):
    return plain_call(kernel, *args, **options)


def plain_call(kernel, out_shape, specs, operands, scratch=(), limit=20, flops=10**8):
    one = not isinstance(out_shape, (list, tuple))
    return pl.pallas_call(
        kernel,
        out_shape=out_shape,
        in_specs=specs,
        out_specs=VMEM if one else tuple(VMEM for _ in out_shape),
        scratch_shapes=list(scratch),
        compiler_params=pltpu.CompilerParams(vmem_limit_bytes=limit << 20),
        cost_estimate=pl.CostEstimate(flops=flops, bytes_accessed=10**6, transcendentals=0),
    )(*operands)


def shape_of(*dims, dtype=jnp.bfloat16):
    return jax.ShapeDtypeStruct(dims, dtype)


def run_copies(copies):
    for copy in copies:
        copy.start()
    for copy in copies:
        copy.wait()


def pack_env_kernel(chain_count, spread, env_ref, out_ref, sem):
    first = place(lax.axis_index("chain"), chain_count) * spread
    before = jnp.maximum(first - 1, 0)
    copies = []

    def add(source, target):
        copies.append(pltpu.make_async_copy(source, target, sem.at[len(copies)]))

    for bond in range(env_ref.shape[0]):
        add(env_ref.at[bond, pl.ds(before, 1)], out_ref.at[bond, pl.ds(0, 1)])
        add(env_ref.at[bond, pl.ds(first, spread)], out_ref.at[bond, pl.ds(1, spread)])
    run_copies(copies)


def pack_site_kernel(chain_count, spread, mps_ref, proj_ref, matrix_ref, *refs):
    out_refs, sem = refs[:-1], refs[-1]
    chain_pos = lax.axis_index("chain")
    side = lax.rem(lax.axis_index("op"), spread)
    copies = []

    def add(source, target):
        copies.append(pltpu.make_async_copy(source, target, sem.at[len(copies)]))

    rows = held_rows(spread)
    for hop, out_ref in enumerate(out_refs):
        first = place(jnp.bitwise_xor(chain_pos, hop), chain_count) * spread
        start = 0
        for phys_state, offset, downs in MPS_PARTS:
            sector = jnp.maximum(first + side + offset, 0) * DOWN_VALUES
            add(
                mps_ref.at[0, phys_state, pl.ds(sector, downs)],
                out_ref.at[pl.ds(start, downs)],
            )
            start += downs
        for phys_state, offset, downs in PROJ_PARTS:
            base = held_base(first, offset, side, spread)
            start = proj_start(phys_state, spread)
            for down in range(downs):
                add(
                    proj_ref.at[0, phys_state, pl.ds(base, rows), down],
                    out_ref.at[pl.ds(start + down * rows, rows)],
                )
        out_ref[out_ref.shape[0] - 1, : matrix_ref.shape[0]] = matrix_ref[...]
    run_copies(copies)


def mask_kernel(charges, out_ref):
    rows, lanes = out_ref.shape
    bond = rows // PHYS
    row_at = lax.broadcasted_iota(jnp.int32, (rows, lanes), 0)
    lane_at = lax.broadcasted_iota(jnp.int32, (rows, lanes), 1)
    ones = jnp.ones((rows, lanes), jnp.float32)
    for axis, table in enumerate((UP_CHARGE, DOWN_CHARGE)):
        left = jnp.zeros((rows, lanes), jnp.int32)
        right = jnp.zeros((rows, lanes), jnp.int32)
        for index in range(bond):
            value = charges[index, axis]
            left = jnp.where(row_at // PHYS == index, value, left)
            right = jnp.where(lane_at % bond == index, value, right)
        for index in range(PHYS):
            left = left - jnp.where(row_at % PHYS == index, table[index], 0)
            right = right - jnp.where(lane_at // bond == index, table[STATE_ORDER[index]], 0)
        ones = jnp.where(left == right, ones, 0.0)
    out_ref[...] = ones


def prep_kernel(site, chain_count, spread, bond, block, slots, sizes, mask, *refs):
    weight_refs = refs[: slots * spread]
    mps_ref, turned, kron, weights, sem = refs[slots * spread :]
    row = my_row(chain_count, spread)
    side = lax.rem(lax.axis_index("op"), spread)
    slot = jnp.bitwise_xor(lax.axis_index("chain"), site)
    for index in range(slots):
        @pl.when(slot == index)
        def _():
            run_copies(
                [
                    pltpu.make_async_copy(
                        weight_refs[index * spread + turn],
                        weights.at[jnp.bitwise_xor(side, turn)],
                        sem.at[turn],
                    )
                    for turn in range(spread)
                ]
            )

    row_at = lax.broadcasted_iota(jnp.int32, (block, block), 0)
    column_at = lax.broadcasted_iota(jnp.int32, (block, block), 1)
    for index, (phys_state, offset, down) in enumerate(MPS_BLOCKS):
        source = jnp.maximum(row + offset, 0) * DOWN_VALUES + down
        target = row * DOWN_VALUES + down + DOWN_CHARGE[phys_state]
        high = jnp.where(row + offset >= 0, sizes[site, source], 0)
        keep = (row_at < high) & (column_at < sizes[site + 1, target])
        value = weights[side, index]
        mps_ref[index] = jnp.where(keep, value, jnp.zeros_like(value))

    held = held_rows(spread)
    turned[...] = jnp.zeros_like(turned)
    for phys_state, offset, _ in PROJ_PARTS:
        for shift in range(ROW_SHIFTS):
            for target in range(DOWN_VALUES):
                down = target - DOWN_CHARGE[phys_state]
                if down < 0:
                    continue
                wanted = row + offset + shift
                holder = (side + shift) // held
                base = held_base(row - side, offset, holder, spread)
                at = jnp.clip(wanted - base, 0, held - 1)
                at = proj_start(phys_state, spread) + down * held + at
                value = weights[holder, at].T
                inside = (wanted >= 0) & (wanted < UP_VALUES)
                turned[
                    shift * DOWN_VALUES + target,
                    :,
                    phys_state * block : (phys_state + 1) * block,
                ] = jnp.where(inside, value, jnp.zeros_like(value))

    pairs = bond * PHYS
    wide = pairs * GROUP
    matrix = weights[side, weights.shape[1] - 1, :pairs, :].astype(jnp.float32)
    matrix = jnp.where(mask[...] > 0.5, matrix, 0.0).astype(jnp.bfloat16)
    lanes = matrix.shape[1]
    tall = (
        lax.broadcasted_iota(jnp.int32, (wide, pairs), 0) // GROUP
        == lax.broadcasted_iota(jnp.int32, (wide, pairs), 1)
    ).astype(jnp.bfloat16)
    across = (
        lax.broadcasted_iota(jnp.int32, (lanes, wide), 0)
        == lax.broadcasted_iota(jnp.int32, (lanes, wide), 1) // GROUP
    ).astype(jnp.bfloat16)
    spread_out = jnp.dot(tall, matrix, preferred_element_type=jnp.float32).astype(jnp.bfloat16)
    spread_out = jnp.dot(spread_out, across, preferred_element_type=jnp.float32)
    same = (
        lax.broadcasted_iota(jnp.int32, (wide, wide), 0) % GROUP
        == lax.broadcasted_iota(jnp.int32, (wide, wide), 1) % GROUP
    )
    kron[...] = jnp.where(same, spread_out, 0.0).astype(jnp.bfloat16)


def mix(mixed, pieces, right, at):
    block = right.shape[0]
    for first, rows in pieces:
        count = rows.shape[0]
        product = jnp.dot(
            rows.reshape(count * block, block), right, preferred_element_type=jnp.float32
        )
        mixed[pl.ds(at + first, count)] = product.reshape(count, block, block)


def contract(mixed, used, kron, row_at, rows, column_at, store):
    block = mixed.shape[-1]

    def body(index, carry):
        at = pl.multiple_of(index * 2 * GROUP, 2 * GROUP)
        low = mixed[:used, pl.ds(at, GROUP), :].reshape(used * GROUP, block)
        high = mixed[:used, pl.ds(at + GROUP, GROUP), :].reshape(used * GROUP, block)
        right = jnp.concatenate([low, high], axis=1).astype(jnp.bfloat16)
        left = kron[pl.ds(row_at, rows), column_at : column_at + used * GROUP]
        got = jnp.dot(left, right, preferred_element_type=jnp.float32)
        store(
            at,
            got[:, :block].reshape(rows // GROUP, GROUP, block),
            got[:, block:].reshape(rows // GROUP, GROUP, block),
        )
        return carry

    steps = block // (2 * GROUP)
    lax.fori_loop(0, steps, body, 0, unroll=steps)


def pieces_of(env_refs, offset, down, spread, per_chunk):
    if len(env_refs) == 1:
        return [(0, env_refs[0][:, down])]
    op_pos = lax.axis_index("op")
    side = lax.rem(op_pos, spread)
    return [
        (jnp.bitwise_xor(op_pos, index) * per_chunk, ref[:, side + 1 + offset, down])
        for index, ref in enumerate(env_refs)
    ]


def left_rows(pairs, kept_rows, spread):
    if kept_rows == pairs:
        return 0
    layer = lax.axis_index("op") // spread
    return pl.multiple_of(layer * (kept_rows * GROUP), kept_rows * GROUP)


def own_kernel(spread, bond, kept_rows, chunks, mps_ref, kron, *refs):
    env_refs, (out_ref, mixed) = refs[:chunks], refs[chunks:]
    pairs = bond * PHYS
    per_chunk = bond // chunks
    at_row = left_rows(pairs, kept_rows, spread)
    for down in range(DOWN_VALUES):
        mix(mixed, pieces_of(env_refs, 0, down, spread, per_chunk), mps_ref[down], 0)
        used = bond
        if down:
            mix(mixed, pieces_of(env_refs, 0, 0, spread, per_chunk), mps_ref[2], bond)
            used = 2 * bond

        def store(at, low, high):
            out_ref[down, :, pl.ds(at, GROUP), :] = low
            out_ref[down, :, pl.ds(at + GROUP, GROUP), :] = high

        contract(mixed, used, kron, at_row, kept_rows * GROUP, 0, store)


def main_kernel(
    chain_count, spread, bond, kept_rows, chunks, others, charges, mps_ref, turned, kron,
    own_ref, *refs
):
    env_refs, refs = refs[:chunks], refs[chunks:]
    kept_refs, refs = refs[:others], refs[others:]
    mixed, summed, result = refs[-3:]
    out_refs = refs[:-3]
    block = mps_ref.shape[-1]
    pairs = bond * PHYS
    per_chunk = bond // chunks
    row = my_row(chain_count, spread)
    at_row = left_rows(pairs, kept_rows, spread)
    last = kept_rows != pairs
    kept_bonds = kept_rows // PHYS
    layer = lax.axis_index("op") // spread
    for down in range(DOWN_VALUES):
        mix(mixed, pieces_of(env_refs, -1, down, spread, per_chunk), mps_ref[3 + down], 0)
        used = bond
        if down:
            mix(mixed, pieces_of(env_refs, -1, 0, spread, per_chunk), mps_ref[5], bond)
            used = 2 * bond

        def store(at, low, high):
            summed[:, pl.ds(at, GROUP), :] = low + own_ref[down, :, pl.ds(at, GROUP), :]
            summed[:, pl.ds(at + GROUP, GROUP), :] = (
                high + own_ref[down, :, pl.ds(at + GROUP, GROUP), :]
            )

        contract(mixed, used, kron, at_row, kept_rows * GROUP, 2 * bond * GROUP, store)
        for index in range(kept_bonds):
            bond_index = layer * kept_bonds + index if last else index
            up = charges[bond_index, 0]
            target = down + charges[bond_index, 1]
            inside = (
                (row + up >= 0)
                & (row + up < UP_VALUES)
                & (target >= 0)
                & (target < DOWN_VALUES)
            )
            entry = jnp.where(
                inside, (up + 1) * DOWN_VALUES + target, ROW_SHIFTS * DOWN_VALUES
            )
            right = (
                summed[index * PHYS : (index + 1) * PHYS]
                .reshape(PHYS * block, block)
                .astype(jnp.bfloat16)
            )
            value = jnp.dot(turned[entry], right, preferred_element_type=jnp.float32)
            value = value.astype(jnp.bfloat16)
            if last:
                result[index, down] = value
            else:
                out_refs[0][index, down] = value
    if not last:
        count = out_refs[1].shape[0]
        out_refs[1][...] = out_refs[0][pl.ds(layer * count, count)]
        return
    chain_pos = lax.axis_index("chain")
    side = lax.rem(lax.axis_index("op"), spread)
    count = kept_bonds // spread
    sources = list(kept_refs) + [result]
    for hop in range(chain_count):
        target_chain = jnp.bitwise_xor(chain_pos, hop)
        for turn in range(spread):
            first = jnp.bitwise_xor(side, turn) * count
            for source_site, source in enumerate(sources):
                @pl.when(target_chain == source_site)
                def _():
                    out_refs[hop * spread + turn][...] = source[pl.ds(first, count)]


def gather_kernel(chain_count, spread, *refs):
    out_ref = refs[-1]
    chain_pos = lax.axis_index("chain")
    side = lax.rem(lax.axis_index("op"), spread)
    for hop in range(chain_count):
        for turn in range(spread):
            row = place(jnp.bitwise_xor(chain_pos, hop), chain_count) * spread
            row = row + jnp.bitwise_xor(side, turn)
            out_ref[0, :, pl.ds(row * DOWN_VALUES, DOWN_VALUES)] = refs[hop * spread + turn][...]


def sweep(env_in, mps, proj, mpo, mpo_charge, block_sizes):
    chain_count = lax.axis_size("chain")
    op_count = lax.axis_size("op")
    local_bond, sectors, block, _ = env_in.shape
    bond = mpo_charge.shape[0]
    pairs = bond * PHYS
    sites = block_sizes.shape[0] - 1
    spread = UP_VALUES // chain_count
    both = ("chain", "op")
    everyone = [(c, o) for c in range(chain_count) for o in range(op_count)]
    square = (block, block)

    def flat(chain, op):
        return chain * op_count + op

    packed = call(
        functools.partial(pack_env_kernel, chain_count, spread),
        shape_of(local_bond, spread + 1, DOWN_VALUES, *square),
        [HBM],
        [env_in.reshape(local_bond, UP_VALUES, DOWN_VALUES, *square)],
        [pltpu.SemaphoreType.DMA((2 * local_bond,))],
        limit=60,
    )
    received = [packed]
    for hop in range(spread, op_count, spread):
        received.append(lax.ppermute(packed, "op", [(o, o ^ hop) for o in range(op_count)]))
    chunks = []
    for piece in received:
        chunks.append(piece)
        for turn in range(1, spread):
            chunks.append(lax.ppermute(piece, "op", [(o, o ^ turn) for o in range(op_count)]))

    matrix = mpo_matrix(mpo[0])
    matrix = jnp.pad(matrix, ((0, 0), (0, block - matrix.shape[1])))
    blocks = proj_start(None, spread) + 1
    far = chain_count - 1
    moves = chain_count * (len(MPS_PARTS) + sum(part[2] for part in PROJ_PARTS))
    parcels = call(
        functools.partial(pack_site_kernel, chain_count, spread),
        [shape_of(blocks, *square)] * chain_count,
        [HBM, HBM, VMEM],
        [
            mps,
            proj.reshape(1, PHYS, UP_VALUES, DOWN_VALUES, *square),
            matrix,
        ],
        [pltpu.SemaphoreType.DMA((moves,))],
        limit=60,
    )
    weights = [parcels[0]]
    for hop in range(1, far):
        weights.append(
            lax.ppermute(parcels[hop], "chain", [(c, c ^ hop) for c in range(chain_count)])
        )
    weights.append(lax.ppermute(parcels[far], "chain", [(0, far)]))
    weights.append(
        lax.ppermute(parcels[far], "chain", [(c, c ^ far) for c in range(1, chain_count)])
    )
    turned_weights = []
    for piece in weights:
        turned_weights.append(
            [piece]
            + [
                lax.ppermute(piece, "op", [(o, o ^ turn) for o in range(op_count)])
                for turn in range(1, spread)
            ]
        )
    weights = turned_weights
    mask = call(mask_kernel, shape_of(pairs, block, dtype=jnp.float32), [SMEM], [mpo_charge])

    halo = []
    for c, o in everyone:
        at = place(c, chain_count)
        if o % spread < spread - 1:
            halo.append((flat(c, o), flat(c, o + 1)))
        elif at < chain_count - 1:
            halo.append((flat(c, o), flat(ring_chain(at + 1, chain_count), o - spread + 1)))

    keep = local_bond * spread
    kept = []
    own_env = prev_env = chunks
    for site in range(sites):
        last = site == sites - 1
        kept_rows = keep * PHYS if last else pairs
        count = len(own_env)
        masked, turned, kron = call(
            functools.partial(
                prep_kernel, site, chain_count, spread, bond, block, chain_count
            ),
            [
                shape_of(len(MPS_BLOCKS), *square),
                shape_of(ROW_SHIFTS * DOWN_VALUES + 1, block, PHYS * block),
                shape_of(pairs * GROUP, pairs * GROUP),
            ],
            [SMEM, VMEM] + [ANY] * (chain_count * spread),
            [block_sizes, mask]
            + sum(weights[:far], [])
            + weights[far + 1 if site else far],
            [
                pltpu.VMEM((spread, blocks, *square), jnp.bfloat16),
                pltpu.SemaphoreType.DMA((spread,)),
            ],
        )
        own = call(
            functools.partial(own_kernel, spread, bond, kept_rows, count),
            shape_of(DOWN_VALUES, kept_rows, *square, dtype=jnp.float32),
            [VMEM] * (2 + count),
            [masked, kron] + own_env,
            [pltpu.VMEM((2 * bond, *square), jnp.float32)],
        )
        if last:
            out = [shape_of(local_bond, DOWN_VALUES, *square)] * (chain_count * spread)
        else:
            out = [shape_of(bond, DOWN_VALUES, *square), shape_of(keep, DOWN_VALUES, *square)]
        others = kept if last else []
        results = call(
            functools.partial(
                main_kernel, chain_count, spread, bond, kept_rows, count, len(others)
            ),
            out,
            [SMEM] + [VMEM] * (4 + count + len(others)),
            [mpo_charge, masked, turned, kron, own] + prev_env + others,
            [
                pltpu.VMEM((2 * bond, *square), jnp.float32),
                pltpu.VMEM((kept_rows, *square), jnp.float32),
                pltpu.VMEM((keep, DOWN_VALUES, *square), jnp.bfloat16),
            ],
            limit=28,
        )
        if not last:
            kept.append(results[1])
            own_env = [results[0]]
            prev_env = [lax.ppermute(results[0], both, halo)]

    arrived = []
    for hop in range(chain_count):
        for turn in range(spread):
            piece = results[hop * spread + turn]
            if hop or turn:
                piece = lax.ppermute(
                    piece, both, [(flat(c, o), flat(c ^ hop, o ^ turn)) for c, o in everyone]
                )
            arrived.append(piece)
    return call(
        functools.partial(gather_kernel, chain_count, spread),
        shape_of(1, local_bond, sectors, *square),
        [VMEM] * len(arrived),
        arrived,
    )


def solution(mesh):
    return jax.shard_map(
        sweep,
        mesh=mesh,
        in_specs=(
            P("op", None, None, None),
            P("chain", None, None, None, None),
            P("chain", None, None, None, None),
            P("chain", None, None, None, None),
            P(),
            P(),
        ),
        out_specs=P("chain", "op", None, None, None),
        check_vma=False,
    )
```

```python
import functools

import jax
import jax.numpy as jnp
from jax import lax
from jax.experimental import pallas as pl
from jax.experimental.pallas import tpu as pltpu
from jax.sharding import PartitionSpec as P


UP_VALUES = 8
DOWN_VALUES = 2
PHYS = 4

UP_CHARGE = (0, 1, 0, 1)
DOWN_CHARGE = (0, 0, 1, 1)

STATE_ORDER = (0, 2, 1, 3)
MPS_PARTS = ((0, 0, 2), (2, 0, 1), (1, -1, 2), (3, -1, 1))
MPS_BLOCKS = ((0, 0, 0), (0, 0, 1), (2, 0, 0), (1, -1, 0), (1, -1, 1), (3, -1, 0))
ROW_SHIFTS = 3
PROJ_PARTS = ((0, -1, 2), (1, -2, 2), (2, -1, 1), (3, -2, 1))
GROUP = 8


VMEM = pl.BlockSpec(memory_space=pltpu.VMEM)
SMEM = pl.BlockSpec(memory_space=pltpu.SMEM)
ANY = pl.BlockSpec(memory_space=pl.ANY)
HBM = pl.BlockSpec(memory_space=pltpu.HBM)


def ring_chain(position, count):
    turned = (position + count - 1) % count
    return turned ^ (turned >> 1)


def place(chain, count):
    plain = chain ^ (chain >> 1) ^ (chain >> 2)
    return (plain + 1) % count if isinstance(chain, int) else lax.rem(plain + 1, count)


def my_row(chain_count, spread):
    side = lax.rem(lax.axis_index("op"), spread)
    return place(lax.axis_index("chain"), chain_count) * spread + side


def held_rows(spread):
    return -(-(ROW_SHIFTS + spread - 1) // spread)


def held_base(first_row, offset, holder, spread):
    rows = held_rows(spread)
    return jnp.clip(first_row + offset + holder * rows, 0, UP_VALUES - rows)


def proj_start(phys_state, spread):
    start = len(MPS_BLOCKS)
    for part_state, _, downs in PROJ_PARTS:
        if part_state == phys_state:
            return start
        start += held_rows(spread) * downs
    return start


def mpo_matrix(site_mpo):
    bond = site_mpo.shape[0]
    ordered = jnp.stack([site_mpo[:, state] for state in STATE_ORDER], axis=1)
    return jnp.transpose(ordered, (2, 3, 1, 0)).reshape(bond * PHYS, PHYS * bond)


def call(kernel, *args, **options):
    return plain_call(kernel, *args, **options)


def plain_call(kernel, out_shape, specs, operands, scratch=(), limit=20, flops=10**8, place_out=VMEM):
    one = not isinstance(out_shape, (list, tuple))
    return pl.pallas_call(
        kernel,
        out_shape=out_shape,
        in_specs=specs,
        out_specs=place_out if one else tuple(place_out for _ in out_shape),
        scratch_shapes=list(scratch),
        compiler_params=pltpu.CompilerParams(vmem_limit_bytes=limit << 20),
        cost_estimate=pl.CostEstimate(flops=flops, bytes_accessed=10**6, transcendentals=0),
    )(*operands)


def shape_of(*dims, dtype=jnp.bfloat16):
    return jax.ShapeDtypeStruct(dims, dtype)


def run_copies(copies):
    for copy in copies:
        copy.start()
    for copy in copies:
        copy.wait()


def pack_env_kernel(chain_count, spread, env_ref, out_ref, sem):
    first = place(lax.axis_index("chain"), chain_count) * spread
    before = jnp.maximum(first - 1, 0)
    copies = []

    def add(source, target):
        copies.append(pltpu.make_async_copy(source, target, sem.at[len(copies)]))

    for bond in range(env_ref.shape[0]):
        add(env_ref.at[bond, pl.ds(before, 1)], out_ref.at[bond, pl.ds(0, 1)])
        add(env_ref.at[bond, pl.ds(first, spread)], out_ref.at[bond, pl.ds(1, spread)])
    run_copies(copies)


def pack_site_kernel(chain_count, spread, first_hop, mps_ref, proj_ref, *refs):
    out_refs, sem = refs[:-1], refs[-1]
    chain_pos = lax.axis_index("chain")
    side = lax.rem(lax.axis_index("op"), spread)
    is_last = (chain_pos == chain_count - 1).astype(jnp.int32)
    copies = []

    def add(source, target):
        copies.append(pltpu.make_async_copy(source, target, sem.at[len(copies)]))

    rows = held_rows(spread)
    for hop, out_ref in enumerate(out_refs, first_hop):
        first = place(jnp.bitwise_xor(chain_pos, hop), chain_count) * spread
        start = 0
        for phys_state, offset, downs in MPS_PARTS:
            late = is_last if offset else 0
            sector = jnp.maximum(first + side + offset + late, 0) * DOWN_VALUES
            add(
                mps_ref.at[0, phys_state, pl.ds(sector, downs)],
                out_ref.at[pl.ds(start, downs)],
            )
            start += downs
        for phys_state, offset, downs in PROJ_PARTS:
            base = held_base(first, offset, side, spread)
            start = proj_start(phys_state, spread)
            for down in range(downs):
                add(
                    proj_ref.at[0, phys_state, pl.ds(base, rows), down],
                    out_ref.at[pl.ds(start + down * rows, rows)],
                )
    run_copies(copies)


def pack_extra_kernel(chain_count, spread, proj_ref, *refs):
    out_refs, sem = refs[:-1], refs[-1]
    copies = []
    for hop, out_ref in enumerate(out_refs):
        first = place(jnp.bitwise_xor(lax.axis_index("chain"), hop), chain_count) * spread
        start = 0
        for phys_state, offset, downs in PROJ_PARTS:
            at = jnp.minimum(first + offset + spread + ROW_SHIFTS - 1, UP_VALUES - 1)
            copies.append(
                pltpu.make_async_copy(
                    proj_ref.at[0, phys_state, at, pl.ds(0, downs)],
                    out_ref.at[pl.ds(start, downs)],
                    sem.at[len(copies)],
                )
            )
            start += downs
    run_copies(copies)


def mask_kernel(charges, out_ref):
    rows, lanes = out_ref.shape
    bond = rows // PHYS
    row_at = lax.broadcasted_iota(jnp.int32, (rows, lanes), 0)
    lane_at = lax.broadcasted_iota(jnp.int32, (rows, lanes), 1)
    ones = jnp.ones((rows, lanes), jnp.float32)
    for axis, table in enumerate((UP_CHARGE, DOWN_CHARGE)):
        left = jnp.zeros((rows, lanes), jnp.int32)
        right = jnp.zeros((rows, lanes), jnp.int32)
        for index in range(bond):
            value = charges[index, axis]
            left = jnp.where(row_at // PHYS == index, value, left)
            right = jnp.where(lane_at % bond == index, value, right)
        for index in range(PHYS):
            left = left - jnp.where(row_at % PHYS == index, table[index], 0)
            right = right - jnp.where(lane_at // bond == index, table[STATE_ORDER[index]], 0)
        ones = jnp.where(left == right, ones, 0.0)
    out_ref[...] = ones


def turn_blocks(turned, row, side, spread, block, read, read_extra=None):
    held = held_rows(spread)
    turned[...] = jnp.zeros_like(turned)
    extra = 0
    for phys_state, offset, downs in PROJ_PARTS:
        for shift in range(ROW_SHIFTS):
            for target in range(DOWN_VALUES):
                down = target - DOWN_CHARGE[phys_state]
                if down < 0:
                    continue
                wanted = row + offset + shift
                holder = jnp.minimum((side + shift) // held, spread - 1)
                base = held_base(row - side, offset, holder, spread)
                at = jnp.clip(wanted - base, 0, held - 1)
                value = read(holder, proj_start(phys_state, spread) + down * held + at)
                if read_extra is not None and shift == ROW_SHIFTS - 1:
                    beyond = side + shift >= spread + ROW_SHIFTS - 1
                    value = jnp.where(beyond, read_extra(extra + down), value)
                inside = (wanted >= 0) & (wanted < UP_VALUES)
                turned[
                    shift * DOWN_VALUES + target,
                    :,
                    phys_state * block : (phys_state + 1) * block,
                ] = jnp.where(inside, value.T, jnp.zeros_like(value))
        extra += downs


def prep_kernel(site, last, chain_count, spread, bond, block, slots, sizes, mask, *refs):
    matrix_refs, refs = refs[:slots], refs[slots:]
    weight_refs, refs = refs[: slots * spread], refs[slots * spread :]
    extra_refs, refs = (refs[:slots], refs[slots:]) if last else ((), refs)
    mps_ref, turned, kron = refs[:3]
    weights, sem = refs[-2:]
    row = my_row(chain_count, spread)
    side = lax.rem(lax.axis_index("op"), spread)
    slot = jnp.bitwise_xor(lax.axis_index("chain"), site)
    for index in range(slots):
        @pl.when(slot == index)
        def _():
            run_copies(
                [
                    pltpu.make_async_copy(
                        weight_refs[index * spread + turn],
                        weights.at[jnp.bitwise_xor(side, turn)],
                        sem.at[turn],
                    )
                    for turn in range(spread)
                ]
            )

    row_at = lax.broadcasted_iota(jnp.int32, (block, block), 0)
    column_at = lax.broadcasted_iota(jnp.int32, (block, block), 1)
    for index, (phys_state, offset, down) in enumerate(MPS_BLOCKS):
        late = 1 if last and offset else 0
        source = row + offset + late
        target = jnp.minimum(row + late, UP_VALUES - 1)
        high = sizes[site, jnp.maximum(source, 0) * DOWN_VALUES + down]
        wide = sizes[site + 1, target * DOWN_VALUES + down + DOWN_CHARGE[phys_state]]
        keep = (row_at < jnp.where(source >= 0, high, 0)) & (column_at < wide)
        value = weights[side, index]
        mps_ref[index] = jnp.where(keep, value, jnp.zeros_like(value))

    def read(holder, at):
        return weights[holder, at]

    turn_blocks(turned, row, side, spread, block, read)
    if last:

        def read_extra(at):
            value = extra_refs[0][at]
            for index in range(1, slots):
                value = jnp.where(slot == index, extra_refs[index][at], value)
            return value

        turn_blocks(refs[3], row + 1, side + 1, spread, block, read, read_extra)

    pairs = bond * PHYS
    wide = pairs * GROUP
    matrix = matrix_refs[0][...].astype(jnp.float32)
    for index in range(1, slots):
        matrix = jnp.where(slot == index, matrix_refs[index][...].astype(jnp.float32), matrix)
    matrix = jnp.where(mask[...] > 0.5, matrix, 0.0).astype(jnp.bfloat16)
    lanes = matrix.shape[1]
    tall = (
        lax.broadcasted_iota(jnp.int32, (wide, pairs), 0) // GROUP
        == lax.broadcasted_iota(jnp.int32, (wide, pairs), 1)
    ).astype(jnp.bfloat16)
    across = (
        lax.broadcasted_iota(jnp.int32, (lanes, wide), 0)
        == lax.broadcasted_iota(jnp.int32, (lanes, wide), 1) // GROUP
    ).astype(jnp.bfloat16)
    spread_out = jnp.dot(tall, matrix, preferred_element_type=jnp.float32).astype(jnp.bfloat16)
    spread_out = jnp.dot(spread_out, across, preferred_element_type=jnp.float32)
    same = (
        lax.broadcasted_iota(jnp.int32, (wide, wide), 0) % GROUP
        == lax.broadcasted_iota(jnp.int32, (wide, wide), 1) % GROUP
    )
    kron[...] = jnp.where(same, spread_out, 0.0).astype(jnp.bfloat16)


def mix(env_refs, offset, mps_ref, spread, bond, flat, deep, flat_at, deep_at):
    block = mps_ref.shape[-1]
    first_block = 0 if offset == 0 else len(MPS_BLOCKS) // 2
    level, falling = mps_ref[first_block], mps_ref[first_block + 2]
    right = jnp.concatenate([level, falling], axis=1)
    per_chunk = bond // len(env_refs)
    for index, ref in enumerate(env_refs):
        if len(env_refs) == 1:
            first, rows = 0, (ref[:, 0], ref[:, 1])
        else:
            op_pos = lax.axis_index("op")
            first = jnp.bitwise_xor(op_pos, index) * per_chunk
            at = lax.rem(op_pos, spread) + 1 + offset
            rows = (ref[:, at, 0], ref[:, at, 1])
        low, high = (
            jnp.dot(
                part.reshape(per_chunk * block, block), other, preferred_element_type=jnp.float32
            )
            for part, other in zip(rows, (right, mps_ref[first_block + 1]))
        )
        shape = (per_chunk, block, block)
        flat[pl.ds(flat_at + first, per_chunk)] = low[:, :block].reshape(shape)
        deep[pl.ds(deep_at + bond + first, per_chunk)] = low[:, block:].reshape(shape)
        deep[pl.ds(deep_at + first, per_chunk)] = high.reshape(shape)


def contract(mixed, left, store):
    block = mixed.shape[-1]
    rows, columns = left.shape
    used = columns // GROUP

    def body(index, carry):
        at = pl.multiple_of(index * 2 * GROUP, 2 * GROUP)
        low = mixed[:used, pl.ds(at, GROUP), :].reshape(columns, block)
        high = mixed[:used, pl.ds(at + GROUP, GROUP), :].reshape(columns, block)
        right = jnp.concatenate([low, high], axis=1).astype(jnp.bfloat16)
        got = jnp.dot(left, right, preferred_element_type=jnp.float32)
        store(
            at,
            got[:, :block].reshape(rows // GROUP, GROUP, block),
            got[:, block:].reshape(rows // GROUP, GROUP, block),
        )
        return carry

    steps = block // (2 * GROUP)
    lax.fori_loop(0, steps, body, 0, unroll=steps)


def left_rows(pairs, kept_rows, spread):
    if kept_rows == pairs:
        return pl.ds(0, pairs * GROUP)
    layer = lax.axis_index("op") // spread
    return pl.ds(pl.multiple_of(layer * (kept_rows * GROUP), kept_rows * GROUP), kept_rows * GROUP)


def own_kernel(spread, bond, mps_ref, kron, env_ref, out_ref, flat, deep):
    mix([env_ref], 0, mps_ref, spread, bond, flat, deep, 0, 0)
    for down, (mixed, states) in enumerate(((flat, 1), (deep, 2))):

        def store(at, low, high):
            out_ref[down, :, pl.ds(at, GROUP), :] = low
            out_ref[down, :, pl.ds(at + GROUP, GROUP), :] = high

        contract(mixed, kron[:, : states * bond * GROUP], store)


def project(down, row, kept_bonds, first_bond, charges, turned, summed, write):
    block = summed.shape[-1]
    for index in range(kept_bonds):
        bond_index = first_bond + index
        up = charges[bond_index, 0]
        target = down + charges[bond_index, 1]
        inside = (row + up >= 0) & (row + up < UP_VALUES) & (target >= 0) & (target < DOWN_VALUES)
        entry = jnp.where(inside, (up + 1) * DOWN_VALUES + target, ROW_SHIFTS * DOWN_VALUES)
        right = (
            summed[index * PHYS : (index + 1) * PHYS]
            .reshape(PHYS * block, block)
            .astype(jnp.bfloat16)
        )
        value = jnp.dot(turned[entry], right, preferred_element_type=jnp.float32)
        write(index, value)


def keep_part(spread, out_ref, keep_ref):
    count = keep_ref.shape[0]
    keep_ref[...] = out_ref[pl.ds(lax.axis_index("op") // spread * count, count)]


def first_kernel(chain_count, spread, bond, chunks, charges, mps_ref, turned, kron, *refs):
    env_refs, (out_ref, keep_ref, flat, deep, summed) = refs[:chunks], refs[chunks:]
    row = my_row(chain_count, spread)
    mix(env_refs, 0, mps_ref, spread, bond, flat, deep, 0, 0)
    mix(env_refs, -1, mps_ref, spread, bond, flat, deep, bond, 2 * bond)
    step = bond * GROUP
    level = jnp.concatenate([kron[:, :step], kron[:, 2 * step : 3 * step]], axis=1)
    for down, (mixed, left) in enumerate(((flat, level), (deep, kron[...]))):

        def store(at, low, high):
            summed[:, pl.ds(at, GROUP), :] = low
            summed[:, pl.ds(at + GROUP, GROUP), :] = high

        def write(index, value):
            out_ref[index, down] = value.astype(jnp.bfloat16)

        contract(mixed, left, store)
        project(down, row, bond, 0, charges, turned, summed, write)
    keep_part(spread, out_ref, keep_ref)


def main_kernel(
    chain_count, spread, bond, charges, mps_ref, turned, kron, own_ref, env_ref,
    out_ref, keep_ref, flat, deep, summed
):
    row = my_row(chain_count, spread)
    half = 2 * bond * GROUP
    mix([env_ref], -1, mps_ref, spread, bond, flat, deep, 0, 0)
    for down, (mixed, states) in enumerate(((flat, 1), (deep, 2))):

        def store(at, low, high):
            summed[:, pl.ds(at, GROUP), :] = low + own_ref[down, :, pl.ds(at, GROUP), :]
            summed[:, pl.ds(at + GROUP, GROUP), :] = (
                high + own_ref[down, :, pl.ds(at + GROUP, GROUP), :]
            )

        def write(index, value):
            out_ref[index, down] = value.astype(jnp.bfloat16)

        contract(mixed, kron[:, half : half + states * bond * GROUP], store)
        project(down, row, bond, 0, charges, turned, summed, write)
    keep_part(spread, out_ref, keep_ref)


def part_kernel(
    chain_count, spread, bond, ahead, charges, mps_ref, turned, kron, env_ref, out_ref,
    flat, deep, summed
):
    row = my_row(chain_count, spread) + ahead
    kept_bonds = out_ref.shape[0]
    rows = left_rows(bond * PHYS, kept_bonds * PHYS, spread)
    start = ahead * 2 * bond * GROUP
    first_bond = lax.axis_index("op") // spread * kept_bonds
    mix([env_ref], -ahead, mps_ref, spread, bond, flat, deep, 0, 0)
    for down, (mixed, states) in enumerate(((flat, 1), (deep, 2))):

        def store(at, low, high):
            summed[:, pl.ds(at, GROUP), :] = low
            summed[:, pl.ds(at + GROUP, GROUP), :] = high

        def write(index, value):
            out_ref[index, down] = value.astype(out_ref.dtype)

        contract(mixed, kron[rows, start : start + states * bond * GROUP], store)
        project(down, row, kept_bonds, first_bond, charges, turned, summed, write)


def sort_kernel(chain_count, spread, own_ref, before_ref, *refs):
    kept_refs, refs = refs[: chain_count - 1], refs[chain_count - 1 :]
    out_refs, result = refs[:-1], refs[-1]
    result[...] = (own_ref[...] + before_ref[...].astype(jnp.float32)).astype(jnp.bfloat16)
    chain_pos = lax.axis_index("chain")
    side = lax.rem(lax.axis_index("op"), spread)
    count = result.shape[0] // spread
    sources = list(kept_refs) + [result]
    for hop in range(chain_count):
        target_chain = jnp.bitwise_xor(chain_pos, hop)
        for turn in range(spread):
            first = jnp.bitwise_xor(side, turn) * count
            for source_site, source in enumerate(sources):
                @pl.when(target_chain == source_site)
                def _():
                    out_refs[hop * spread + turn][...] = source[pl.ds(first, count)]


def gather_kernel(chain_count, spread, *refs):
    out_ref = refs[-1]
    chain_pos = lax.axis_index("chain")
    side = lax.rem(lax.axis_index("op"), spread)
    for hop in range(chain_count):
        for turn in range(spread):
            row = place(jnp.bitwise_xor(chain_pos, hop), chain_count) * spread
            row = row + jnp.bitwise_xor(side, turn)
            out_ref[0, :, pl.ds(row * DOWN_VALUES, DOWN_VALUES)] = refs[hop * spread + turn][...]


def sweep(env_in, mps, proj, mpo, mpo_charge, block_sizes):
    chain_count = lax.axis_size("chain")
    op_count = lax.axis_size("op")
    local_bond, sectors, block, _ = env_in.shape
    bond = mpo_charge.shape[0]
    pairs = bond * PHYS
    sites = block_sizes.shape[0] - 1
    spread = UP_VALUES // chain_count
    both = ("chain", "op")
    everyone = [(c, o) for c in range(chain_count) for o in range(op_count)]
    square = (block, block)

    def flat(chain, op):
        return chain * op_count + op

    packed = call(
        functools.partial(pack_env_kernel, chain_count, spread),
        shape_of(local_bond, spread + 1, DOWN_VALUES, *square),
        [HBM],
        [env_in.reshape(local_bond, UP_VALUES, DOWN_VALUES, *square)],
        [pltpu.SemaphoreType.DMA((2 * local_bond,))],
        limit=60,
        place_out=VMEM,
    )
    own_packed = call(
        functools.partial(pack_env_kernel, chain_count, spread),
        shape_of(local_bond, spread + 1, DOWN_VALUES, *square),
        [ANY],
        [env_in.reshape(local_bond, UP_VALUES, DOWN_VALUES, *square)],
        [pltpu.SemaphoreType.DMA((2 * local_bond,))],
    )
    received = [packed]
    for hop in range(spread, op_count, spread):
        received.append(lax.ppermute(packed, "op", [(o, o ^ hop) for o in range(op_count)]))
    chunks = []
    for piece in received:
        chunks.append(piece)
        for turn in range(1, spread):
            chunks.append(lax.ppermute(piece, "op", [(o, o ^ turn) for o in range(op_count)]))
    chunks[0] = own_packed

    blocks = proj_start(None, spread)
    far = chain_count - 1
    moves = len(MPS_PARTS) + sum(part[2] for part in PROJ_PARTS)
    tensors = [mps, proj.reshape(1, PHYS, UP_VALUES, DOWN_VALUES, *square)]
    parcels = call(
        functools.partial(pack_site_kernel, chain_count, spread, 1),
        [shape_of(blocks, *square)] * far,
        [HBM, HBM],
        tensors,
        [pltpu.SemaphoreType.DMA((moves * far,))],
        limit=60,
        place_out=VMEM,
    )
    parcels = call(
        functools.partial(pack_site_kernel, chain_count, spread, 0),
        [shape_of(blocks, *square)],
        [ANY, ANY],
        tensors,
        [pltpu.SemaphoreType.DMA((moves,))],
    ) + parcels
    weights = [parcels[0]]
    for hop in range(1, far):
        weights.append(
            lax.ppermute(parcels[hop], "chain", [(c, c ^ hop) for c in range(chain_count)])
        )
    weights.append(lax.ppermute(parcels[far], "chain", [(0, far)]))
    weights.append(
        lax.ppermute(parcels[far], "chain", [(c, c ^ far) for c in range(1, chain_count)])
    )
    turned_weights = []
    for piece in weights:
        turned_weights.append(
            [piece]
            + [
                lax.ppermute(piece, "op", [(o, o ^ turn) for o in range(op_count)])
                for turn in range(1, spread)
            ]
        )
    weights = turned_weights
    matrix = mpo_matrix(mpo[0])
    matrix = jnp.pad(matrix, ((0, 0), (0, block - matrix.shape[1])))
    matrices = [matrix]
    for hop in range(1, chain_count):
        matrices.append(lax.ppermute(matrix, "chain", [(c, c ^ hop) for c in range(chain_count)]))
    extra_count = sum(part[2] for part in PROJ_PARTS)
    extras = list(call(
        functools.partial(pack_extra_kernel, chain_count, spread),
        [shape_of(extra_count, *square)] * chain_count,
        [ANY],
        tensors[1:],
        [pltpu.SemaphoreType.DMA((chain_count * len(PROJ_PARTS),))],
    ))
    middle = chain_count // 2
    for hop in range(1, chain_count):
        first_stop = far ^ (middle if hop == far else hop)
        extras[hop] = lax.ppermute(extras[hop], "chain", [(far, first_stop)])
    extras[far] = lax.ppermute(extras[far], "chain", [(far ^ middle, 0)])
    mask = call(mask_kernel, shape_of(pairs, block, dtype=jnp.float32), [SMEM], [mpo_charge])

    halo = []
    for c, o in everyone:
        at = place(c, chain_count)
        if o % spread < spread - 1:
            halo.append((flat(c, o), flat(c, o + 1)))
        elif at < chain_count - 1:
            halo.append((flat(c, o), flat(ring_chain(at + 1, chain_count), o - spread + 1)))

    keep = local_bond * spread
    kept = []
    mixed_scratch = [
        pltpu.VMEM((bond, *square), jnp.float32),
        pltpu.VMEM((2 * bond, *square), jnp.float32),
    ]
    table = shape_of(ROW_SHIFTS * DOWN_VALUES + 1, block, PHYS * block)
    full = [shape_of(bond, DOWN_VALUES, *square), shape_of(keep, DOWN_VALUES, *square)]
    for site in range(sites):
        last = site == sites - 1
        masked, turned, kron, *more = call(
            functools.partial(
                prep_kernel, site, last, chain_count, spread, bond, block, chain_count
            ),
            [
                shape_of(len(MPS_BLOCKS), *square),
                table,
                shape_of(pairs * GROUP, pairs * GROUP),
            ]
            + [table] * last,
            [SMEM, VMEM]
            + [VMEM] * chain_count
            + [ANY] * (chain_count * spread)
            + [VMEM] * (chain_count * last),
            [block_sizes, mask]
            + matrices
            + sum(weights[:far], [])
            + weights[far + 1 if site else far]
            + extras * last,
            [
                pltpu.VMEM((spread, blocks, *square), jnp.bfloat16),
                pltpu.SemaphoreType.DMA((spread,)),
            ],
        )
        if site == 0:
            finished, part = call(
                functools.partial(first_kernel, chain_count, spread, bond, len(chunks)),
                full,
                [SMEM] + [VMEM] * (3 + len(chunks)),
                [mpo_charge, masked, turned, kron] + chunks,
                [
                    pltpu.VMEM((2 * bond, *square), jnp.float32),
                    pltpu.VMEM((4 * bond, *square), jnp.float32),
                    pltpu.VMEM((pairs, *square), jnp.float32),
                ],
                limit=28,
            )
            kept.append(part)
        elif not last:
            before = lax.ppermute(finished, both, halo)
            own = call(
                functools.partial(own_kernel, spread, bond),
                shape_of(DOWN_VALUES, pairs, *square, dtype=jnp.float32),
                [VMEM] * 3,
                [masked, kron, finished],
                mixed_scratch,
            )
            finished, part = call(
                functools.partial(main_kernel, chain_count, spread, bond),
                full,
                [SMEM] + [VMEM] * 5,
                [mpo_charge, masked, turned, kron, own, before],
                mixed_scratch + [pltpu.VMEM((pairs, *square), jnp.float32)],
                limit=28,
            )
            kept.append(part)
        else:
            parts = [
                call(
                    functools.partial(part_kernel, chain_count, spread, bond, ahead),
                    shape_of(keep, DOWN_VALUES, *square, dtype=dtype),
                    [SMEM] + [VMEM] * 4,
                    [mpo_charge, masked, entries, kron, finished],
                    mixed_scratch + [pltpu.VMEM((keep * PHYS, *square), jnp.float32)],
                    limit=28,
                )
                for ahead, entries, dtype in (
                    (1, more[0], jnp.bfloat16),
                    (0, turned, jnp.float32),
                )
            ]
            before = lax.ppermute(parts[0], both, halo)
            results = call(
                functools.partial(sort_kernel, chain_count, spread),
                [shape_of(local_bond, DOWN_VALUES, *square)] * (chain_count * spread),
                [VMEM] * (2 + len(kept)),
                [parts[1], before] + kept,
                [pltpu.VMEM((keep, DOWN_VALUES, *square), jnp.bfloat16)],
            )

    arrived = []
    for hop in range(chain_count):
        for turn in range(spread):
            piece = results[hop * spread + turn]
            if hop or turn:
                piece = lax.ppermute(
                    piece, both, [(flat(c, o), flat(c ^ hop, o ^ turn)) for c, o in everyone]
                )
            arrived.append(piece)
    return call(
        functools.partial(gather_kernel, chain_count, spread),
        shape_of(1, local_bond, sectors, *square),
        [VMEM] * len(arrived),
        arrived,
    )


def solution(mesh):
    return jax.shard_map(
        sweep,
        mesh=mesh,
        in_specs=(
            P("op", None, None, None),
            P("chain", None, None, None, None),
            P("chain", None, None, None, None),
            P("chain", None, None, None, None),
            P(),
            P(),
        ),
        out_specs=P("chain", "op", None, None, None),
        check_vma=False,
    )
```

```python
import functools

import jax
import jax.numpy as jnp
from jax import lax
from jax.experimental import pallas as pl
from jax.experimental.pallas import tpu as pltpu
from jax.sharding import PartitionSpec as P


UP_VALUES = 8
DOWN_VALUES = 2
PHYS = 4

UP_CHARGE = (0, 1, 0, 1)
DOWN_CHARGE = (0, 0, 1, 1)

STATE_ORDER = (0, 2, 1, 3)
MPS_PARTS = ((0, 0, 2), (2, 0, 1), (1, -1, 2), (3, -1, 1))
MPS_BLOCKS = ((0, 0, 0), (0, 0, 1), (2, 0, 0), (1, -1, 0), (1, -1, 1), (3, -1, 0))
ROW_SHIFTS = 3
PROJ_PARTS = ((0, -1, 2), (1, -2, 2), (2, -1, 1), (3, -2, 1))
GROUP = 8


VMEM = pl.BlockSpec(memory_space=pltpu.VMEM)
SMEM = pl.BlockSpec(memory_space=pltpu.SMEM)
ANY = pl.BlockSpec(memory_space=pl.ANY)
HBM = pl.BlockSpec(memory_space=pltpu.HBM)


def ring_chain(position, count):
    turned = (position + count - 1) % count
    return turned ^ (turned >> 1)


def place(chain, count):
    plain = chain ^ (chain >> 1) ^ (chain >> 2)
    return (plain + 1) % count if isinstance(chain, int) else lax.rem(plain + 1, count)


def my_row(chain_count, spread):
    side = lax.rem(lax.axis_index("op"), spread)
    return place(lax.axis_index("chain"), chain_count) * spread + side


def held_rows(spread):
    return -(-(ROW_SHIFTS + spread - 1) // spread)


def held_base(first_row, offset, holder, spread):
    rows = held_rows(spread)
    return jnp.clip(first_row + offset + holder * rows, 0, UP_VALUES - rows)


def proj_start(phys_state, spread):
    start = len(MPS_BLOCKS)
    for part_state, _, downs in PROJ_PARTS:
        if part_state == phys_state:
            return start
        start += held_rows(spread) * downs
    return start


def mpo_matrix(site_mpo):
    bond = site_mpo.shape[0]
    ordered = jnp.stack([site_mpo[:, state] for state in STATE_ORDER], axis=1)
    return jnp.transpose(ordered, (2, 3, 1, 0)).reshape(bond * PHYS, PHYS * bond)


def call(kernel, *args, **options):
    return plain_call(kernel, *args, **options)


def plain_call(kernel, out_shape, specs, operands, scratch=(), limit=20, flops=10**8, place_out=VMEM):
    one = not isinstance(out_shape, (list, tuple))
    return pl.pallas_call(
        kernel,
        out_shape=out_shape,
        in_specs=specs,
        out_specs=place_out if one else tuple(place_out for _ in out_shape),
        scratch_shapes=list(scratch),
        compiler_params=pltpu.CompilerParams(vmem_limit_bytes=limit << 20),
        cost_estimate=pl.CostEstimate(flops=flops, bytes_accessed=10**6, transcendentals=0),
    )(*operands)


def shape_of(*dims, dtype=jnp.bfloat16):
    return jax.ShapeDtypeStruct(dims, dtype)


def run_copies(copies):
    for copy in copies:
        copy.start()
    for copy in copies:
        copy.wait()


def pack_env_kernel(chain_count, spread, env_ref, out_ref, sem):
    first = place(lax.axis_index("chain"), chain_count) * spread
    before = jnp.maximum(first - 1, 0)
    copies = []

    def add(source, target):
        copies.append(pltpu.make_async_copy(source, target, sem.at[len(copies)]))

    for bond in range(env_ref.shape[0]):
        add(env_ref.at[bond, pl.ds(before, 1)], out_ref.at[bond, pl.ds(0, 1)])
        add(env_ref.at[bond, pl.ds(first, spread)], out_ref.at[bond, pl.ds(1, spread)])
    run_copies(copies)


def pack_site_kernel(chain_count, spread, first_hop, mps_ref, proj_ref, *refs):
    out_refs, sem = refs[:-1], refs[-1]
    chain_pos = lax.axis_index("chain")
    side = lax.rem(lax.axis_index("op"), spread)
    is_last = (chain_pos == chain_count - 1).astype(jnp.int32)
    copies = []

    def add(source, target):
        copies.append(pltpu.make_async_copy(source, target, sem.at[len(copies)]))

    rows = held_rows(spread)
    for hop, out_ref in enumerate(out_refs, first_hop):
        first = place(jnp.bitwise_xor(chain_pos, hop), chain_count) * spread
        start = 0
        for phys_state, offset, downs in MPS_PARTS:
            late = is_last if offset else 0
            sector = jnp.maximum(first + side + offset + late, 0) * DOWN_VALUES
            add(
                mps_ref.at[0, phys_state, pl.ds(sector, downs)],
                out_ref.at[pl.ds(start, downs)],
            )
            start += downs
        for phys_state, offset, downs in PROJ_PARTS:
            base = held_base(first, offset, side, spread)
            start = proj_start(phys_state, spread)
            for down in range(downs):
                add(
                    proj_ref.at[0, phys_state, pl.ds(base, rows), down],
                    out_ref.at[pl.ds(start + down * rows, rows)],
                )
    run_copies(copies)


def pick_extra_kernel(last_site, chain_count, spread, *refs):
    weight_refs, out_ref, sem = refs[:-2], refs[-2], refs[-1]
    chain_pos = lax.axis_index("chain")
    slot = jnp.bitwise_xor(chain_pos, last_site)
    first = place(chain_pos, chain_count) * spread
    held = held_rows(spread)
    holder = (ROW_SHIFTS - 1) // held
    for index, weight_ref in enumerate(weight_refs):
        @pl.when(slot == index)
        def _():
            copies = []
            for phys_state, offset, downs in PROJ_PARTS:
                base = held_base(first, offset, holder, spread)
                at = jnp.clip(first + offset + ROW_SHIFTS - 1 - base, 0, held - 1)
                for down in range(downs):
                    copies.append(
                        pltpu.make_async_copy(
                            weight_ref.at[proj_start(phys_state, spread) + down * held + at],
                            out_ref.at[len(copies)],
                            sem.at[len(copies)],
                        )
                    )
            run_copies(copies)


def mask_kernel(charges, out_ref):
    rows, lanes = out_ref.shape
    bond = rows // PHYS
    row_at = lax.broadcasted_iota(jnp.int32, (rows, lanes), 0)
    lane_at = lax.broadcasted_iota(jnp.int32, (rows, lanes), 1)
    ones = jnp.ones((rows, lanes), jnp.float32)
    for axis, table in enumerate((UP_CHARGE, DOWN_CHARGE)):
        left = jnp.zeros((rows, lanes), jnp.int32)
        right = jnp.zeros((rows, lanes), jnp.int32)
        for index in range(bond):
            value = charges[index, axis]
            left = jnp.where(row_at // PHYS == index, value, left)
            right = jnp.where(lane_at % bond == index, value, right)
        for index in range(PHYS):
            left = left - jnp.where(row_at % PHYS == index, table[index], 0)
            right = right - jnp.where(lane_at // bond == index, table[STATE_ORDER[index]], 0)
        ones = jnp.where(left == right, ones, 0.0)
    out_ref[...] = ones


def turn_blocks(turned, row, side, spread, block, read, read_extra=None):
    held = held_rows(spread)
    turned[...] = jnp.zeros_like(turned)
    extra = 0
    for phys_state, offset, downs in PROJ_PARTS:
        for shift in range(ROW_SHIFTS):
            for target in range(DOWN_VALUES):
                down = target - DOWN_CHARGE[phys_state]
                if down < 0:
                    continue
                wanted = row + offset + shift
                holder = jnp.minimum((side + shift) // held, spread - 1)
                base = held_base(row - side, offset, holder, spread)
                at = jnp.clip(wanted - base, 0, held - 1)
                value = read(holder, proj_start(phys_state, spread) + down * held + at)
                if read_extra is not None and shift == ROW_SHIFTS - 1:
                    beyond = side + shift >= spread + ROW_SHIFTS - 1
                    value = jnp.where(beyond, read_extra(extra + down), value)
                inside = (wanted >= 0) & (wanted < UP_VALUES)
                turned[
                    shift * DOWN_VALUES + target,
                    :,
                    phys_state * block : (phys_state + 1) * block,
                ] = jnp.where(inside, value.T, jnp.zeros_like(value))
        extra += downs


def prep_kernel(site, last, chain_count, spread, bond, block, slots, sizes, mask, *refs):
    matrix_refs, refs = refs[:slots], refs[slots:]
    weight_refs, refs = refs[: slots * spread], refs[slots * spread :]
    extra_ref, refs = (refs[0], refs[1:]) if last else (None, refs)
    mps_ref, turned, kron = refs[:3]
    weights, sem = refs[-2:]
    row = my_row(chain_count, spread)
    side = lax.rem(lax.axis_index("op"), spread)
    slot = jnp.bitwise_xor(lax.axis_index("chain"), site)
    for index in range(slots):
        @pl.when(slot == index)
        def _():
            run_copies(
                [
                    pltpu.make_async_copy(
                        weight_refs[index * spread + turn],
                        weights.at[jnp.bitwise_xor(side, turn)],
                        sem.at[turn],
                    )
                    for turn in range(spread)
                ]
            )

    row_at = lax.broadcasted_iota(jnp.int32, (block, block), 0)
    column_at = lax.broadcasted_iota(jnp.int32, (block, block), 1)
    for index, (phys_state, offset, down) in enumerate(MPS_BLOCKS):
        late = 1 if last and offset else 0
        source = row + offset + late
        target = jnp.minimum(row + late, UP_VALUES - 1)
        high = sizes[site, jnp.maximum(source, 0) * DOWN_VALUES + down]
        wide = sizes[site + 1, target * DOWN_VALUES + down + DOWN_CHARGE[phys_state]]
        keep = (row_at < jnp.where(source >= 0, high, 0)) & (column_at < wide)
        value = weights[side, index]
        mps_ref[index] = jnp.where(keep, value, jnp.zeros_like(value))

    def read(holder, at):
        return weights[holder, at]

    turn_blocks(turned, row, side, spread, block, read)
    if last:

        turn_blocks(refs[3], row + 1, side + 1, spread, block, read, lambda at: extra_ref[at])

    pairs = bond * PHYS
    wide = pairs * GROUP
    matrix = matrix_refs[0][...].astype(jnp.float32)
    for index in range(1, slots):
        matrix = jnp.where(slot == index, matrix_refs[index][...].astype(jnp.float32), matrix)
    matrix = jnp.where(mask[...] > 0.5, matrix, 0.0).astype(jnp.bfloat16)
    lanes = matrix.shape[1]
    tall = (
        lax.broadcasted_iota(jnp.int32, (wide, pairs), 0) // GROUP
        == lax.broadcasted_iota(jnp.int32, (wide, pairs), 1)
    ).astype(jnp.bfloat16)
    across = (
        lax.broadcasted_iota(jnp.int32, (lanes, wide), 0)
        == lax.broadcasted_iota(jnp.int32, (lanes, wide), 1) // GROUP
    ).astype(jnp.bfloat16)
    spread_out = jnp.dot(tall, matrix, preferred_element_type=jnp.float32).astype(jnp.bfloat16)
    spread_out = jnp.dot(spread_out, across, preferred_element_type=jnp.float32)
    same = (
        lax.broadcasted_iota(jnp.int32, (wide, wide), 0) % GROUP
        == lax.broadcasted_iota(jnp.int32, (wide, wide), 1) % GROUP
    )
    kron[...] = jnp.where(same, spread_out, 0.0).astype(jnp.bfloat16)


def mix(env_refs, offset, mps_ref, spread, bond, flat, deep, flat_at, deep_at):
    block = mps_ref.shape[-1]
    first_block = 0 if offset == 0 else len(MPS_BLOCKS) // 2
    level, falling = mps_ref[first_block], mps_ref[first_block + 2]
    right = jnp.concatenate([level, falling], axis=1)
    per_chunk = bond // len(env_refs)
    for index, ref in enumerate(env_refs):
        if len(env_refs) == 1:
            first, rows = 0, (ref[:, 0], ref[:, 1])
        else:
            op_pos = lax.axis_index("op")
            first = jnp.bitwise_xor(op_pos, index) * per_chunk
            at = lax.rem(op_pos, spread) + 1 + offset
            rows = (ref[:, at, 0], ref[:, at, 1])
        low, high = (
            jnp.dot(
                part.reshape(per_chunk * block, block), other, preferred_element_type=jnp.float32
            )
            for part, other in zip(rows, (right, mps_ref[first_block + 1]))
        )
        shape = (per_chunk, block, block)
        flat[pl.ds(flat_at + first, per_chunk)] = low[:, :block].reshape(shape)
        deep[pl.ds(deep_at + bond + first, per_chunk)] = low[:, block:].reshape(shape)
        deep[pl.ds(deep_at + first, per_chunk)] = high.reshape(shape)


def contract(mixed, left, store):
    block = mixed.shape[-1]
    rows, columns = left.shape
    used = columns // GROUP

    def body(index, carry):
        at = pl.multiple_of(index * 2 * GROUP, 2 * GROUP)
        low = mixed[:used, pl.ds(at, GROUP), :].reshape(columns, block)
        high = mixed[:used, pl.ds(at + GROUP, GROUP), :].reshape(columns, block)
        right = jnp.concatenate([low, high], axis=1).astype(jnp.bfloat16)
        got = jnp.dot(left, right, preferred_element_type=jnp.float32)
        store(
            at,
            got[:, :block].reshape(rows // GROUP, GROUP, block),
            got[:, block:].reshape(rows // GROUP, GROUP, block),
        )
        return carry

    steps = block // (2 * GROUP)
    lax.fori_loop(0, steps, body, 0, unroll=steps)


def left_rows(pairs, kept_rows, spread):
    if kept_rows == pairs:
        return pl.ds(0, pairs * GROUP)
    layer = lax.axis_index("op") // spread
    return pl.ds(pl.multiple_of(layer * (kept_rows * GROUP), kept_rows * GROUP), kept_rows * GROUP)


def own_kernel(spread, bond, mps_ref, kron, env_ref, out_ref, flat, deep):
    mix([env_ref], 0, mps_ref, spread, bond, flat, deep, 0, 0)
    for down, (mixed, states) in enumerate(((flat, 1), (deep, 2))):

        def store(at, low, high):
            out_ref[down, :, pl.ds(at, GROUP), :] = low
            out_ref[down, :, pl.ds(at + GROUP, GROUP), :] = high

        contract(mixed, kron[:, : states * bond * GROUP], store)


def project(down, row, kept_bonds, first_bond, charges, turned, summed, write):
    block = summed.shape[-1]
    for index in range(kept_bonds):
        bond_index = first_bond + index
        up = charges[bond_index, 0]
        target = down + charges[bond_index, 1]
        inside = (row + up >= 0) & (row + up < UP_VALUES) & (target >= 0) & (target < DOWN_VALUES)
        entry = jnp.where(inside, (up + 1) * DOWN_VALUES + target, ROW_SHIFTS * DOWN_VALUES)
        right = (
            summed[index * PHYS : (index + 1) * PHYS]
            .reshape(PHYS * block, block)
            .astype(jnp.bfloat16)
        )
        value = jnp.dot(turned[entry], right, preferred_element_type=jnp.float32)
        write(index, value)


def keep_part(spread, out_ref, keep_ref):
    count = keep_ref.shape[0]
    keep_ref[...] = out_ref[pl.ds(lax.axis_index("op") // spread * count, count)]


def first_kernel(chain_count, spread, bond, chunks, charges, mps_ref, turned, kron, *refs):
    env_refs, (out_ref, keep_ref, flat, deep, summed) = refs[:chunks], refs[chunks:]
    row = my_row(chain_count, spread)
    mix(env_refs, 0, mps_ref, spread, bond, flat, deep, 0, 0)
    mix(env_refs, -1, mps_ref, spread, bond, flat, deep, bond, 2 * bond)
    step = bond * GROUP
    level = jnp.concatenate([kron[:, :step], kron[:, 2 * step : 3 * step]], axis=1)
    for down, (mixed, left) in enumerate(((flat, level), (deep, kron[...]))):

        def store(at, low, high):
            summed[:, pl.ds(at, GROUP), :] = low
            summed[:, pl.ds(at + GROUP, GROUP), :] = high

        def write(index, value):
            out_ref[index, down] = value.astype(jnp.bfloat16)

        contract(mixed, left, store)
        project(down, row, bond, 0, charges, turned, summed, write)
    keep_part(spread, out_ref, keep_ref)


def main_kernel(
    chain_count, spread, bond, outer, charges, mps_ref, turned, kron, own_ref, env_ref, *refs
):
    inner_ref, refs = (refs[0], refs[1:]) if outer and spread > 1 else (None, refs)
    out_ref, refs = refs[0], refs[1:]
    keep_ref, refs = (refs[0], refs[1:]) if outer else (None, refs)
    flat, deep, summed = refs
    row = my_row(chain_count, spread)
    half = 2 * bond * GROUP
    from_outside = lax.rem(lax.axis_index("op"), spread) == 0

    def compute():
        mix([env_ref], -1, mps_ref, spread, bond, flat, deep, 0, 0)
        for down, (mixed, states) in enumerate(((flat, 1), (deep, 2))):

            def store(at, low, high):
                summed[:, pl.ds(at, GROUP), :] = low + own_ref[down, :, pl.ds(at, GROUP), :]
                summed[:, pl.ds(at + GROUP, GROUP), :] = (
                    high + own_ref[down, :, pl.ds(at + GROUP, GROUP), :]
                )

            def write(index, value):
                out_ref[index, down] = value.astype(jnp.bfloat16)

            contract(mixed, kron[:, half : half + states * bond * GROUP], store)
            project(down, row, bond, 0, charges, turned, summed, write)

    pl.when(from_outside if outer else jnp.logical_not(from_outside))(compute)
    if inner_ref is not None:

        @pl.when(jnp.logical_not(from_outside))
        def _():
            out_ref[...] = inner_ref[...]

    if outer:
        keep_part(spread, out_ref, keep_ref)


def part_kernel(
    chain_count, spread, bond, ahead, charges, mps_ref, turned, kron, env_ref, out_ref,
    flat, deep, summed
):
    row = my_row(chain_count, spread) + ahead
    kept_bonds = out_ref.shape[0]
    rows = left_rows(bond * PHYS, kept_bonds * PHYS, spread)
    start = ahead * 2 * bond * GROUP
    first_bond = lax.axis_index("op") // spread * kept_bonds
    mix([env_ref], -ahead, mps_ref, spread, bond, flat, deep, 0, 0)
    for down, (mixed, states) in enumerate(((flat, 1), (deep, 2))):

        def store(at, low, high):
            summed[:, pl.ds(at, GROUP), :] = low
            summed[:, pl.ds(at + GROUP, GROUP), :] = high

        def write(index, value):
            out_ref[index, down] = value.astype(out_ref.dtype)

        contract(mixed, kron[rows, start : start + states * bond * GROUP], store)
        project(down, row, kept_bonds, first_bond, charges, turned, summed, write)


def sort_kernel(chain_count, spread, own_ref, before_ref, *refs):
    kept_refs, refs = refs[: chain_count - 1], refs[chain_count - 1 :]
    out_refs, result = refs[:-1], refs[-1]
    result[...] = (own_ref[...] + before_ref[...].astype(jnp.float32)).astype(jnp.bfloat16)
    chain_pos = lax.axis_index("chain")
    side = lax.rem(lax.axis_index("op"), spread)
    count = result.shape[0] // spread
    sources = list(kept_refs) + [result]
    for hop in range(chain_count):
        target_chain = jnp.bitwise_xor(chain_pos, hop)
        for turn in range(spread):
            first = jnp.bitwise_xor(side, turn) * count
            for source_site, source in enumerate(sources):
                @pl.when(target_chain == source_site)
                def _():
                    out_refs[hop * spread + turn][...] = source[pl.ds(first, count)]


def gather_kernel(chain_count, spread, *refs):
    out_ref = refs[-1]
    chain_pos = lax.axis_index("chain")
    side = lax.rem(lax.axis_index("op"), spread)
    for hop in range(chain_count):
        for turn in range(spread):
            row = place(jnp.bitwise_xor(chain_pos, hop), chain_count) * spread
            row = row + jnp.bitwise_xor(side, turn)
            out_ref[0, :, pl.ds(row * DOWN_VALUES, DOWN_VALUES)] = refs[hop * spread + turn][...]


def sweep(env_in, mps, proj, mpo, mpo_charge, block_sizes):
    chain_count = lax.axis_size("chain")
    op_count = lax.axis_size("op")
    local_bond, sectors, block, _ = env_in.shape
    bond = mpo_charge.shape[0]
    pairs = bond * PHYS
    sites = block_sizes.shape[0] - 1
    spread = UP_VALUES // chain_count
    both = ("chain", "op")
    everyone = [(c, o) for c in range(chain_count) for o in range(op_count)]
    square = (block, block)

    def flat(chain, op):
        return chain * op_count + op

    packed = call(
        functools.partial(pack_env_kernel, chain_count, spread),
        shape_of(local_bond, spread + 1, DOWN_VALUES, *square),
        [HBM],
        [env_in.reshape(local_bond, UP_VALUES, DOWN_VALUES, *square)],
        [pltpu.SemaphoreType.DMA((2 * local_bond,))],
        limit=60,
        place_out=VMEM,
    )
    own_packed = call(
        functools.partial(pack_env_kernel, chain_count, spread),
        shape_of(local_bond, spread + 1, DOWN_VALUES, *square),
        [ANY],
        [env_in.reshape(local_bond, UP_VALUES, DOWN_VALUES, *square)],
        [pltpu.SemaphoreType.DMA((2 * local_bond,))],
    )
    received = [packed]
    for hop in range(spread, op_count, spread):
        received.append(lax.ppermute(packed, "op", [(o, o ^ hop) for o in range(op_count)]))
    chunks = []
    for piece in received:
        chunks.append(piece)
        for turn in range(1, spread):
            chunks.append(lax.ppermute(piece, "op", [(o, o ^ turn) for o in range(op_count)]))
    chunks[0] = own_packed

    blocks = proj_start(None, spread)
    far = chain_count - 1
    moves = len(MPS_PARTS) + sum(part[2] for part in PROJ_PARTS)
    tensors = [mps, proj.reshape(1, PHYS, UP_VALUES, DOWN_VALUES, *square)]
    parcels = call(
        functools.partial(pack_site_kernel, chain_count, spread, 1),
        [shape_of(blocks, *square)] * far,
        [HBM, HBM],
        tensors,
        [pltpu.SemaphoreType.DMA((moves * far,))],
        limit=60,
        place_out=VMEM,
    )
    parcels = call(
        functools.partial(pack_site_kernel, chain_count, spread, 0),
        [shape_of(blocks, *square)],
        [ANY, ANY],
        tensors,
        [pltpu.SemaphoreType.DMA((moves,))],
    ) + parcels
    weights = [parcels[0]]
    for hop in range(1, far):
        weights.append(
            lax.ppermute(parcels[hop], "chain", [(c, c ^ hop) for c in range(chain_count)])
        )
    weights.append(lax.ppermute(parcels[far], "chain", [(0, far)]))
    weights.append(
        lax.ppermute(parcels[far], "chain", [(c, c ^ far) for c in range(1, chain_count)])
    )
    turned_weights = []
    for piece in weights:
        turned_weights.append(
            [piece]
            + [
                lax.ppermute(piece, "op", [(o, o ^ turn) for o in range(op_count)])
                for turn in range(1, spread)
            ]
        )
    weights = turned_weights
    matrix = mpo_matrix(mpo[0])
    matrix = jnp.pad(matrix, ((0, 0), (0, block - matrix.shape[1])))
    matrices = [matrix]
    for hop in range(1, chain_count):
        matrices.append(lax.ppermute(matrix, "chain", [(c, c ^ hop) for c in range(chain_count)]))
    mask = call(mask_kernel, shape_of(pairs, block, dtype=jnp.float32), [SMEM], [mpo_charge])

    inner_halo, outer_halo = [], []
    for c, o in everyone:
        at = place(c, chain_count)
        if o % spread < spread - 1:
            inner_halo.append((flat(c, o), flat(c, o + 1)))
        elif at < chain_count - 1:
            outer_halo.append(
                (flat(c, o), flat(ring_chain(at + 1, chain_count), o - spread + 1))
            )
    halo = inner_halo + outer_halo

    keep = local_bond * spread
    kept = []
    turn = (spread - 1) ^ ((ROW_SHIFTS - 1) // held_rows(spread))
    late = weights[:far] + [weights[far + 1]]
    extra_count = sum(part[2] for part in PROJ_PARTS)
    extra = call(
        functools.partial(pick_extra_kernel, sites - 1, chain_count, spread),
        shape_of(extra_count, *square),
        [ANY] * chain_count,
        [pieces[turn] for pieces in late],
        [pltpu.SemaphoreType.DMA((extra_count,))],
    )
    extra = lax.ppermute(
        extra,
        both,
        [
            (flat(ring_chain(at + 1, chain_count), o), flat(ring_chain(at, chain_count), o))
            for at in range(chain_count - 1)
            for o in range(spread - 1, op_count, spread)
        ],
    )
    mixed_scratch = [
        pltpu.VMEM((bond, *square), jnp.float32),
        pltpu.VMEM((2 * bond, *square), jnp.float32),
    ]
    table = shape_of(ROW_SHIFTS * DOWN_VALUES + 1, block, PHYS * block)
    full = [shape_of(bond, DOWN_VALUES, *square), shape_of(keep, DOWN_VALUES, *square)]
    for site in range(sites):
        last = site == sites - 1
        masked, turned, kron, *more = call(
            functools.partial(
                prep_kernel, site, last, chain_count, spread, bond, block, chain_count
            ),
            [
                shape_of(len(MPS_BLOCKS), *square),
                table,
                shape_of(pairs * GROUP, pairs * GROUP),
            ]
            + [table] * last,
            [SMEM, VMEM]
            + [VMEM] * chain_count
            + [ANY] * (chain_count * spread)
            + [VMEM] * last,
            [block_sizes, mask]
            + matrices
            + sum(weights[:far], [])
            + weights[far + 1 if site else far]
            + [extra] * last,
            [
                pltpu.VMEM((spread, blocks, *square), jnp.bfloat16),
                pltpu.SemaphoreType.DMA((spread,)),
            ],
        )
        if site == 0:
            finished, part = call(
                functools.partial(first_kernel, chain_count, spread, bond, len(chunks)),
                full,
                [SMEM] + [VMEM] * (3 + len(chunks)),
                [mpo_charge, masked, turned, kron] + chunks,
                [
                    pltpu.VMEM((2 * bond, *square), jnp.float32),
                    pltpu.VMEM((4 * bond, *square), jnp.float32),
                    pltpu.VMEM((pairs, *square), jnp.float32),
                ],
                limit=28,
            )
            kept.append(part)
            leaving = finished
        elif not last:
            own = call(
                functools.partial(own_kernel, spread, bond),
                shape_of(DOWN_VALUES, pairs, *square, dtype=jnp.float32),
                [VMEM] * 3,
                [masked, kron, finished],
                mixed_scratch,
            )
            shared = [mpo_charge, masked, turned, kron, own]
            scratch = mixed_scratch + [pltpu.VMEM((pairs, *square), jnp.float32)]
            outside = lax.ppermute(leaving, both, outer_halo)
            passed = []
            if spread > 1:
                inside = lax.ppermute(finished, both, inner_halo)
                passed.append(
                    call(
                        functools.partial(main_kernel, chain_count, spread, bond, False),
                        full[0],
                        [SMEM] + [VMEM] * 5,
                        shared + [inside],
                        scratch,
                        limit=28,
                    )
                )
            finished, part = call(
                functools.partial(main_kernel, chain_count, spread, bond, True),
                full,
                [SMEM] + [VMEM] * (5 + len(passed)),
                shared + [outside] + passed,
                scratch,
                limit=28,
            )
            leaving = passed[0] if spread == 2 else finished
            kept.append(part)
        else:
            parts = [
                call(
                    functools.partial(part_kernel, chain_count, spread, bond, ahead),
                    shape_of(keep, DOWN_VALUES, *square, dtype=dtype),
                    [SMEM] + [VMEM] * 4,
                    [mpo_charge, masked, entries, kron, finished],
                    mixed_scratch + [pltpu.VMEM((keep * PHYS, *square), jnp.float32)],
                    limit=28,
                )
                for ahead, entries, dtype in (
                    (1, more[0], jnp.bfloat16),
                    (0, turned, jnp.float32),
                )
            ]
            before = lax.ppermute(parts[0], both, halo)
            results = call(
                functools.partial(sort_kernel, chain_count, spread),
                [shape_of(local_bond, DOWN_VALUES, *square)] * (chain_count * spread),
                [VMEM] * (2 + len(kept)),
                [parts[1], before] + kept,
                [pltpu.VMEM((keep, DOWN_VALUES, *square), jnp.bfloat16)],
            )

    arrived = []
    for hop in range(chain_count):
        for turn in range(spread):
            piece = results[hop * spread + turn]
            if hop or turn:
                piece = lax.ppermute(
                    piece, both, [(flat(c, o), flat(c ^ hop, o ^ turn)) for c, o in everyone]
                )
            arrived.append(piece)
    return call(
        functools.partial(gather_kernel, chain_count, spread),
        shape_of(1, local_bond, sectors, *square),
        [VMEM] * len(arrived),
        arrived,
    )


def solution(mesh):
    return jax.shard_map(
        sweep,
        mesh=mesh,
        in_specs=(
            P("op", None, None, None),
            P("chain", None, None, None, None),
            P("chain", None, None, None, None),
            P("chain", None, None, None, None),
            P(),
            P(),
        ),
        out_specs=P("chain", "op", None, None, None),
        check_vma=False,
    )
```

```python
import functools

import jax
import jax.numpy as jnp
from jax import lax
from jax.experimental import pallas as pl
from jax.experimental.pallas import tpu as pltpu
from jax.sharding import PartitionSpec as P


UP_VALUES = 8
DOWN_VALUES = 2
PHYS = 4

UP_CHARGE = (0, 1, 0, 1)
DOWN_CHARGE = (0, 0, 1, 1)

STATE_ORDER = (0, 2, 1, 3)
MPS_PARTS = ((0, 0, 2), (2, 0, 1), (1, -1, 2), (3, -1, 1))
MPS_BLOCKS = ((0, 0, 0), (0, 0, 1), (2, 0, 0), (1, -1, 0), (1, -1, 1), (3, -1, 0))
ROW_SHIFTS = 3
PROJ_PARTS = ((0, -1, 2), (1, -2, 2), (2, -1, 1), (3, -2, 1))
GROUP = 8


VMEM = pl.BlockSpec(memory_space=pltpu.VMEM)
SMEM = pl.BlockSpec(memory_space=pltpu.SMEM)
ANY = pl.BlockSpec(memory_space=pl.ANY)
HBM = pl.BlockSpec(memory_space=pltpu.HBM)


def ring_chain(position, count):
    turned = (position + count - 1) % count
    return turned ^ (turned >> 1)


def place(chain, count):
    plain = chain ^ (chain >> 1) ^ (chain >> 2)
    return (plain + 1) % count if isinstance(chain, int) else lax.rem(plain + 1, count)


def my_row(chain_count, spread):
    side = lax.rem(lax.axis_index("op"), spread)
    return place(lax.axis_index("chain"), chain_count) * spread + side


def held_rows(spread):
    return -(-(ROW_SHIFTS + spread - 1) // spread)


def held_base(first_row, offset, holder, spread):
    rows = held_rows(spread)
    return jnp.clip(first_row + offset + holder * rows, 0, UP_VALUES - rows)


def proj_start(phys_state, spread):
    start = len(MPS_BLOCKS)
    for part_state, _, downs in PROJ_PARTS:
        if part_state == phys_state:
            return start
        start += held_rows(spread) * downs
    return start


def mpo_matrix(site_mpo):
    bond = site_mpo.shape[0]
    ordered = jnp.stack([site_mpo[:, state] for state in STATE_ORDER], axis=1)
    return jnp.transpose(ordered, (2, 3, 1, 0)).reshape(bond * PHYS, PHYS * bond)


def call(kernel, *args, **options):
    return plain_call(kernel, *args, **options)


def plain_call(kernel, out_shape, specs, operands, scratch=(), limit=20, flops=10**8, place_out=VMEM):
    one = not isinstance(out_shape, (list, tuple))
    return pl.pallas_call(
        kernel,
        out_shape=out_shape,
        in_specs=specs,
        out_specs=place_out if one else tuple(place_out for _ in out_shape),
        scratch_shapes=list(scratch),
        compiler_params=pltpu.CompilerParams(vmem_limit_bytes=limit << 20),
        cost_estimate=pl.CostEstimate(flops=flops, bytes_accessed=10**6, transcendentals=0),
    )(*operands)


def shape_of(*dims, dtype=jnp.bfloat16):
    return jax.ShapeDtypeStruct(dims, dtype)


def run_copies(copies):
    for copy in copies:
        copy.start()
    for copy in copies:
        copy.wait()


def pack_env_kernel(chain_count, spread, env_ref, out_ref, sem):
    first = place(lax.axis_index("chain"), chain_count) * spread
    before = jnp.maximum(first - 1, 0)
    copies = []

    def add(source, target):
        copies.append(pltpu.make_async_copy(source, target, sem.at[len(copies)]))

    for bond in range(env_ref.shape[0]):
        add(env_ref.at[bond, pl.ds(before, 1)], out_ref.at[bond, pl.ds(0, 1)])
        add(env_ref.at[bond, pl.ds(first, spread)], out_ref.at[bond, pl.ds(1, spread)])
    run_copies(copies)


def pack_site_kernel(chain_count, spread, first_hop, mps_ref, proj_ref, *refs):
    out_refs, sem = refs[:-1], refs[-1]
    chain_pos = lax.axis_index("chain")
    side = lax.rem(lax.axis_index("op"), spread)
    is_last = (chain_pos == chain_count - 1).astype(jnp.int32)
    copies = []

    def add(source, target):
        copies.append(pltpu.make_async_copy(source, target, sem.at[len(copies)]))

    rows = held_rows(spread)
    for hop, out_ref in enumerate(out_refs, first_hop):
        first = place(jnp.bitwise_xor(chain_pos, hop), chain_count) * spread
        start = 0
        for phys_state, offset, downs in MPS_PARTS:
            late = is_last if offset else 0
            sector = jnp.maximum(first + side + offset + late, 0) * DOWN_VALUES
            add(
                mps_ref.at[0, phys_state, pl.ds(sector, downs)],
                out_ref.at[pl.ds(start, downs)],
            )
            start += downs
        for phys_state, offset, downs in PROJ_PARTS:
            base = held_base(first, offset, side, spread)
            start = proj_start(phys_state, spread)
            for down in range(downs):
                add(
                    proj_ref.at[0, phys_state, pl.ds(base, rows), down],
                    out_ref.at[pl.ds(start + down * rows, rows)],
                )
    run_copies(copies)


def pick_extra_kernel(last_site, chain_count, spread, *refs):
    weight_refs, out_ref, sem = refs[:-2], refs[-2], refs[-1]
    chain_pos = lax.axis_index("chain")
    slot = jnp.bitwise_xor(chain_pos, last_site)
    first = place(chain_pos, chain_count) * spread
    held = held_rows(spread)
    holder = (ROW_SHIFTS - 1) // held
    for index, weight_ref in enumerate(weight_refs):
        @pl.when(slot == index)
        def _():
            copies = []
            for phys_state, offset, downs in PROJ_PARTS:
                base = held_base(first, offset, holder, spread)
                at = jnp.clip(first + offset + ROW_SHIFTS - 1 - base, 0, held - 1)
                for down in range(downs):
                    copies.append(
                        pltpu.make_async_copy(
                            weight_ref.at[proj_start(phys_state, spread) + down * held + at],
                            out_ref.at[len(copies)],
                            sem.at[len(copies)],
                        )
                    )
            run_copies(copies)


def mask_kernel(charges, out_ref):
    rows, lanes = out_ref.shape
    bond = rows // PHYS
    row_at = lax.broadcasted_iota(jnp.int32, (rows, lanes), 0)
    lane_at = lax.broadcasted_iota(jnp.int32, (rows, lanes), 1)
    ones = jnp.ones((rows, lanes), jnp.float32)
    for axis, table in enumerate((UP_CHARGE, DOWN_CHARGE)):
        left = jnp.zeros((rows, lanes), jnp.int32)
        right = jnp.zeros((rows, lanes), jnp.int32)
        for index in range(bond):
            value = charges[index, axis]
            left = jnp.where(row_at // PHYS == index, value, left)
            right = jnp.where(lane_at % bond == index, value, right)
        for index in range(PHYS):
            left = left - jnp.where(row_at % PHYS == index, table[index], 0)
            right = right - jnp.where(lane_at // bond == index, table[STATE_ORDER[index]], 0)
        ones = jnp.where(left == right, ones, 0.0)
    out_ref[...] = ones


def turn_blocks(turned, row, side, spread, block, read, read_extra=None):
    held = held_rows(spread)
    turned[...] = jnp.zeros_like(turned)
    extra = 0
    for phys_state, offset, downs in PROJ_PARTS:
        for shift in range(ROW_SHIFTS):
            for target in range(DOWN_VALUES):
                down = target - DOWN_CHARGE[phys_state]
                if down < 0:
                    continue
                wanted = row + offset + shift
                holder = jnp.minimum((side + shift) // held, spread - 1)
                base = held_base(row - side, offset, holder, spread)
                at = jnp.clip(wanted - base, 0, held - 1)
                value = read(holder, proj_start(phys_state, spread) + down * held + at)
                if read_extra is not None and shift == ROW_SHIFTS - 1:
                    beyond = side + shift >= spread + ROW_SHIFTS - 1
                    value = jnp.where(beyond, read_extra(extra + down), value)
                inside = (wanted >= 0) & (wanted < UP_VALUES)
                turned[
                    shift * DOWN_VALUES + target,
                    :,
                    phys_state * block : (phys_state + 1) * block,
                ] = jnp.where(inside, value.T, jnp.zeros_like(value))
        extra += downs


def prep_kernel(site, last, chain_count, spread, bond, block, slots, sizes, mask, *refs):
    matrix_refs, refs = refs[:slots], refs[slots:]
    weight_refs, refs = refs[: slots * spread], refs[slots * spread :]
    extra_ref, refs = (refs[0], refs[1:]) if last else (None, refs)
    mps_ref, turned, kron = refs[:3]
    weights, sem = refs[-2:]
    row = my_row(chain_count, spread)
    side = lax.rem(lax.axis_index("op"), spread)
    slot = jnp.bitwise_xor(lax.axis_index("chain"), site)
    for index in range(slots):
        @pl.when(slot == index)
        def _():
            run_copies(
                [
                    pltpu.make_async_copy(
                        weight_refs[index * spread + turn],
                        weights.at[jnp.bitwise_xor(side, turn)],
                        sem.at[turn],
                    )
                    for turn in range(spread)
                ]
            )

    row_at = lax.broadcasted_iota(jnp.int32, (block, block), 0)
    column_at = lax.broadcasted_iota(jnp.int32, (block, block), 1)
    for index, (phys_state, offset, down) in enumerate(MPS_BLOCKS):
        late = 1 if last and offset else 0
        source = row + offset + late
        target = jnp.minimum(row + late, UP_VALUES - 1)
        high = sizes[site, jnp.maximum(source, 0) * DOWN_VALUES + down]
        wide = sizes[site + 1, target * DOWN_VALUES + down + DOWN_CHARGE[phys_state]]
        keep = (row_at < jnp.where(source >= 0, high, 0)) & (column_at < wide)
        value = weights[side, index]
        mps_ref[index] = jnp.where(keep, value, jnp.zeros_like(value))

    def read(holder, at):
        return weights[holder, at]

    turn_blocks(turned, row, side, spread, block, read)
    if last:

        turn_blocks(refs[3], row + 1, side + 1, spread, block, read, lambda at: extra_ref[at])

    pairs = bond * PHYS
    wide = pairs * GROUP
    matrix = matrix_refs[0][...].astype(jnp.float32)
    for index in range(1, slots):
        matrix = jnp.where(slot == index, matrix_refs[index][...].astype(jnp.float32), matrix)
    matrix = jnp.where(mask[...] > 0.5, matrix, 0.0).astype(jnp.bfloat16)
    lanes = matrix.shape[1]
    tall = (
        lax.broadcasted_iota(jnp.int32, (wide, pairs), 0) // GROUP
        == lax.broadcasted_iota(jnp.int32, (wide, pairs), 1)
    ).astype(jnp.bfloat16)
    across = (
        lax.broadcasted_iota(jnp.int32, (lanes, wide), 0)
        == lax.broadcasted_iota(jnp.int32, (lanes, wide), 1) // GROUP
    ).astype(jnp.bfloat16)
    spread_out = jnp.dot(tall, matrix, preferred_element_type=jnp.float32).astype(jnp.bfloat16)
    spread_out = jnp.dot(spread_out, across, preferred_element_type=jnp.float32)
    same = (
        lax.broadcasted_iota(jnp.int32, (wide, wide), 0) % GROUP
        == lax.broadcasted_iota(jnp.int32, (wide, wide), 1) % GROUP
    )
    kron[...] = jnp.where(same, spread_out, 0.0).astype(jnp.bfloat16)


def mix(env_refs, offset, mps_ref, spread, bond, flat, deep, flat_at, deep_at):
    block = mps_ref.shape[-1]
    first_block = 0 if offset == 0 else len(MPS_BLOCKS) // 2
    level, falling = mps_ref[first_block], mps_ref[first_block + 2]
    right = jnp.concatenate([level, falling], axis=1)
    per_chunk = bond // len(env_refs)
    for index, ref in enumerate(env_refs):
        if len(env_refs) == 1:
            first, rows = 0, (ref[:, 0], ref[:, 1])
        else:
            op_pos = lax.axis_index("op")
            first = jnp.bitwise_xor(op_pos, index) * per_chunk
            at = lax.rem(op_pos, spread) + 1 + offset
            rows = (ref[:, at, 0], ref[:, at, 1])
        low, high = (
            jnp.dot(
                part.reshape(per_chunk * block, block), other, preferred_element_type=jnp.float32
            )
            for part, other in zip(rows, (right, mps_ref[first_block + 1]))
        )
        shape = (per_chunk, block, block)
        flat[pl.ds(flat_at + first, per_chunk)] = low[:, :block].reshape(shape)
        deep[pl.ds(deep_at + bond + first, per_chunk)] = low[:, block:].reshape(shape)
        deep[pl.ds(deep_at + first, per_chunk)] = high.reshape(shape)


def contract(mixed, left, store):
    block = mixed.shape[-1]
    rows, columns = left.shape
    used = columns // GROUP

    def body(index, carry):
        at = pl.multiple_of(index * 2 * GROUP, 2 * GROUP)
        low = mixed[:used, pl.ds(at, GROUP), :].reshape(columns, block)
        high = mixed[:used, pl.ds(at + GROUP, GROUP), :].reshape(columns, block)
        right = jnp.concatenate([low, high], axis=1).astype(jnp.bfloat16)
        got = jnp.dot(left, right, preferred_element_type=jnp.float32)
        store(
            at,
            got[:, :block].reshape(rows // GROUP, GROUP, block),
            got[:, block:].reshape(rows // GROUP, GROUP, block),
        )
        return carry

    steps = block // (2 * GROUP)
    lax.fori_loop(0, steps, body, 0, unroll=steps)


def left_rows(pairs, kept_rows, spread):
    if kept_rows == pairs:
        return pl.ds(0, pairs * GROUP)
    layer = lax.axis_index("op") // spread
    return pl.ds(pl.multiple_of(layer * (kept_rows * GROUP), kept_rows * GROUP), kept_rows * GROUP)


def own_kernel(spread, bond, mps_ref, kron, env_ref, out_ref, flat, deep):
    mix([env_ref], 0, mps_ref, spread, bond, flat, deep, 0, 0)
    for down, (mixed, states) in enumerate(((flat, 1), (deep, 2))):

        def store(at, low, high):
            out_ref[down, :, pl.ds(at, GROUP), :] = low
            out_ref[down, :, pl.ds(at + GROUP, GROUP), :] = high

        contract(mixed, kron[:, : states * bond * GROUP], store)


def project(down, row, kept_bonds, first_bond, charges, turned, summed, write):
    block = summed.shape[-1]
    for index in range(kept_bonds):
        bond_index = first_bond + index
        up = charges[bond_index, 0]
        target = down + charges[bond_index, 1]
        inside = (row + up >= 0) & (row + up < UP_VALUES) & (target >= 0) & (target < DOWN_VALUES)
        entry = jnp.where(inside, (up + 1) * DOWN_VALUES + target, ROW_SHIFTS * DOWN_VALUES)
        right = (
            summed[index * PHYS : (index + 1) * PHYS]
            .reshape(PHYS * block, block)
            .astype(jnp.bfloat16)
        )
        value = jnp.dot(turned[entry], right, preferred_element_type=jnp.float32)
        write(index, value)


def keep_part(spread, out_ref, keep_ref):
    count = keep_ref.shape[0]
    keep_ref[...] = out_ref[pl.ds(lax.axis_index("op") // spread * count, count)]


def finish_whole(row, bond, charges, turned, kron, flat, deep, summed, out_ref):
    step = bond * GROUP
    level = jnp.concatenate([kron[:, :step], kron[:, 2 * step : 3 * step]], axis=1)
    for down, (mixed, left) in enumerate(((flat, level), (deep, kron[...]))):

        def store(at, low, high):
            summed[:, pl.ds(at, GROUP), :] = low
            summed[:, pl.ds(at + GROUP, GROUP), :] = high

        def write(index, value):
            out_ref[index, down] = value.astype(jnp.bfloat16)

        contract(mixed, left, store)
        project(down, row, bond, 0, charges, turned, summed, write)


def first_kernel(chain_count, spread, bond, chunks, charges, mps_ref, turned, kron, *refs):
    env_refs, (out_ref, keep_ref, flat, deep, summed) = refs[:chunks], refs[chunks:]
    row = my_row(chain_count, spread)
    mix(env_refs, 0, mps_ref, spread, bond, flat, deep, 0, 0)
    mix(env_refs, -1, mps_ref, spread, bond, flat, deep, bond, 2 * bond)
    finish_whole(row, bond, charges, turned, kron, flat, deep, summed, out_ref)
    keep_part(spread, out_ref, keep_ref)


def inner_kernel(
    chain_count, spread, bond, charges, mps_ref, turned, kron, env_ref, inside_ref, out_ref,
    flat, deep, summed
):
    row = my_row(chain_count, spread)

    @pl.when(lax.rem(lax.axis_index("op"), spread) != 0)
    def _():
        mix([env_ref], 0, mps_ref, spread, bond, flat, deep, 0, 0)
        mix([inside_ref], -1, mps_ref, spread, bond, flat, deep, bond, 2 * bond)
        finish_whole(row, bond, charges, turned, kron, flat, deep, summed, out_ref)


def main_kernel(
    chain_count, spread, bond, outer, charges, mps_ref, turned, kron, own_ref, env_ref, *refs
):
    inner_ref, refs = (refs[0], refs[1:]) if outer and spread > 1 else (None, refs)
    out_ref, refs = refs[0], refs[1:]
    keep_ref, refs = (refs[0], refs[1:]) if outer else (None, refs)
    flat, deep, summed = refs
    row = my_row(chain_count, spread)
    half = 2 * bond * GROUP
    from_outside = lax.rem(lax.axis_index("op"), spread) == 0

    def compute():
        mix([env_ref], -1, mps_ref, spread, bond, flat, deep, 0, 0)
        for down, (mixed, states) in enumerate(((flat, 1), (deep, 2))):

            def store(at, low, high):
                summed[:, pl.ds(at, GROUP), :] = low + own_ref[down, :, pl.ds(at, GROUP), :]
                summed[:, pl.ds(at + GROUP, GROUP), :] = (
                    high + own_ref[down, :, pl.ds(at + GROUP, GROUP), :]
                )

            def write(index, value):
                out_ref[index, down] = value.astype(jnp.bfloat16)

            contract(mixed, kron[:, half : half + states * bond * GROUP], store)
            project(down, row, bond, 0, charges, turned, summed, write)

    pl.when(from_outside if outer else jnp.logical_not(from_outside))(compute)
    if inner_ref is not None:

        @pl.when(jnp.logical_not(from_outside))
        def _():
            out_ref[...] = inner_ref[...]

    if outer:
        keep_part(spread, out_ref, keep_ref)


def part_kernel(
    chain_count, spread, bond, ahead, charges, mps_ref, turned, kron, env_ref, out_ref,
    flat, deep, summed
):
    row = my_row(chain_count, spread) + ahead
    kept_bonds = out_ref.shape[0]
    rows = left_rows(bond * PHYS, kept_bonds * PHYS, spread)
    start = ahead * 2 * bond * GROUP
    first_bond = lax.axis_index("op") // spread * kept_bonds
    mix([env_ref], -ahead, mps_ref, spread, bond, flat, deep, 0, 0)
    for down, (mixed, states) in enumerate(((flat, 1), (deep, 2))):

        def store(at, low, high):
            summed[:, pl.ds(at, GROUP), :] = low
            summed[:, pl.ds(at + GROUP, GROUP), :] = high

        def write(index, value):
            out_ref[index, down] = value.astype(out_ref.dtype)

        contract(mixed, kron[rows, start : start + states * bond * GROUP], store)
        project(down, row, kept_bonds, first_bond, charges, turned, summed, write)


def sort_kernel(chain_count, spread, own_ref, before_ref, *refs):
    kept_refs, refs = refs[: chain_count - 1], refs[chain_count - 1 :]
    out_refs, result = refs[:-1], refs[-1]
    result[...] = (own_ref[...] + before_ref[...].astype(jnp.float32)).astype(jnp.bfloat16)
    chain_pos = lax.axis_index("chain")
    side = lax.rem(lax.axis_index("op"), spread)
    count = result.shape[0] // spread
    sources = list(kept_refs) + [result]
    for hop in range(chain_count):
        target_chain = jnp.bitwise_xor(chain_pos, hop)
        for turn in range(spread):
            first = jnp.bitwise_xor(side, turn) * count
            for source_site, source in enumerate(sources):
                @pl.when(target_chain == source_site)
                def _():
                    out_refs[hop * spread + turn][...] = source[pl.ds(first, count)]


def gather_kernel(chain_count, spread, *refs):
    out_ref = refs[-1]
    chain_pos = lax.axis_index("chain")
    side = lax.rem(lax.axis_index("op"), spread)
    for hop in range(chain_count):
        for turn in range(spread):
            row = place(jnp.bitwise_xor(chain_pos, hop), chain_count) * spread
            row = row + jnp.bitwise_xor(side, turn)
            out_ref[0, :, pl.ds(row * DOWN_VALUES, DOWN_VALUES)] = refs[hop * spread + turn][...]


def sweep(env_in, mps, proj, mpo, mpo_charge, block_sizes):
    chain_count = lax.axis_size("chain")
    op_count = lax.axis_size("op")
    local_bond, sectors, block, _ = env_in.shape
    bond = mpo_charge.shape[0]
    pairs = bond * PHYS
    sites = block_sizes.shape[0] - 1
    spread = UP_VALUES // chain_count
    both = ("chain", "op")
    everyone = [(c, o) for c in range(chain_count) for o in range(op_count)]
    square = (block, block)

    def flat(chain, op):
        return chain * op_count + op

    packed = call(
        functools.partial(pack_env_kernel, chain_count, spread),
        shape_of(local_bond, spread + 1, DOWN_VALUES, *square),
        [HBM],
        [env_in.reshape(local_bond, UP_VALUES, DOWN_VALUES, *square)],
        [pltpu.SemaphoreType.DMA((2 * local_bond,))],
        limit=60,
        place_out=VMEM,
    )
    own_packed = call(
        functools.partial(pack_env_kernel, chain_count, spread),
        shape_of(local_bond, spread + 1, DOWN_VALUES, *square),
        [ANY],
        [env_in.reshape(local_bond, UP_VALUES, DOWN_VALUES, *square)],
        [pltpu.SemaphoreType.DMA((2 * local_bond,))],
    )
    received = [packed]
    for hop in range(spread, op_count, spread):
        received.append(lax.ppermute(packed, "op", [(o, o ^ hop) for o in range(op_count)]))
    chunks = []
    for piece in received:
        chunks.append(piece)
        for turn in range(1, spread):
            chunks.append(lax.ppermute(piece, "op", [(o, o ^ turn) for o in range(op_count)]))
    chunks[0] = own_packed

    blocks = proj_start(None, spread)
    far = chain_count - 1
    moves = len(MPS_PARTS) + sum(part[2] for part in PROJ_PARTS)
    tensors = [mps, proj.reshape(1, PHYS, UP_VALUES, DOWN_VALUES, *square)]
    parcels = call(
        functools.partial(pack_site_kernel, chain_count, spread, 1),
        [shape_of(blocks, *square)] * far,
        [HBM, HBM],
        tensors,
        [pltpu.SemaphoreType.DMA((moves * far,))],
        limit=60,
        place_out=VMEM,
    )
    parcels = call(
        functools.partial(pack_site_kernel, chain_count, spread, 0),
        [shape_of(blocks, *square)],
        [ANY, ANY],
        tensors,
        [pltpu.SemaphoreType.DMA((moves,))],
    ) + parcels
    weights = [parcels[0]]
    for hop in range(1, far):
        weights.append(
            lax.ppermute(parcels[hop], "chain", [(c, c ^ hop) for c in range(chain_count)])
        )
    weights.append(lax.ppermute(parcels[far], "chain", [(0, far)]))
    weights.append(
        lax.ppermute(parcels[far], "chain", [(c, c ^ far) for c in range(1, chain_count)])
    )
    turned_weights = []
    for piece in weights:
        turned_weights.append(
            [piece]
            + [
                lax.ppermute(piece, "op", [(o, o ^ turn) for o in range(op_count)])
                for turn in range(1, spread)
            ]
        )
    weights = turned_weights
    matrix = mpo_matrix(mpo[0])
    matrix = jnp.pad(matrix, ((0, 0), (0, block - matrix.shape[1])))
    matrices = [matrix]
    for hop in range(1, chain_count):
        matrices.append(lax.ppermute(matrix, "chain", [(c, c ^ hop) for c in range(chain_count)]))
    mask = call(mask_kernel, shape_of(pairs, block, dtype=jnp.float32), [SMEM], [mpo_charge])

    inner_halo, outer_halo = [], []
    for c, o in everyone:
        at = place(c, chain_count)
        if o % spread < spread - 1:
            inner_halo.append((flat(c, o), flat(c, o + 1)))
        elif at < chain_count - 1:
            outer_halo.append(
                (flat(c, o), flat(ring_chain(at + 1, chain_count), o - spread + 1))
            )
    halo = inner_halo + outer_halo

    keep = local_bond * spread
    kept = []
    turn = (spread - 1) ^ ((ROW_SHIFTS - 1) // held_rows(spread))
    late = weights[:far] + [weights[far + 1]]
    extra_count = sum(part[2] for part in PROJ_PARTS)
    extra = call(
        functools.partial(pick_extra_kernel, sites - 1, chain_count, spread),
        shape_of(extra_count, *square),
        [ANY] * chain_count,
        [pieces[turn] for pieces in late],
        [pltpu.SemaphoreType.DMA((extra_count,))],
    )
    extra = lax.ppermute(
        extra,
        both,
        [
            (flat(ring_chain(at + 1, chain_count), o), flat(ring_chain(at, chain_count), o))
            for at in range(chain_count - 1)
            for o in range(spread - 1, op_count, spread)
        ],
    )
    mixed_scratch = [
        pltpu.VMEM((bond, *square), jnp.float32),
        pltpu.VMEM((2 * bond, *square), jnp.float32),
    ]
    table = shape_of(ROW_SHIFTS * DOWN_VALUES + 1, block, PHYS * block)
    full = [shape_of(bond, DOWN_VALUES, *square), shape_of(keep, DOWN_VALUES, *square)]
    for site in range(sites):
        last = site == sites - 1
        masked, turned, kron, *more = call(
            functools.partial(
                prep_kernel, site, last, chain_count, spread, bond, block, chain_count
            ),
            [
                shape_of(len(MPS_BLOCKS), *square),
                table,
                shape_of(pairs * GROUP, pairs * GROUP),
            ]
            + [table] * last,
            [SMEM, VMEM]
            + [VMEM] * chain_count
            + [ANY] * (chain_count * spread)
            + [VMEM] * last,
            [block_sizes, mask]
            + matrices
            + sum(weights[:far], [])
            + weights[far + 1 if site else far]
            + [extra] * last,
            [
                pltpu.VMEM((spread, blocks, *square), jnp.bfloat16),
                pltpu.SemaphoreType.DMA((spread,)),
            ],
        )
        if site == 0:
            finished, part = call(
                functools.partial(first_kernel, chain_count, spread, bond, len(chunks)),
                full,
                [SMEM] + [VMEM] * (3 + len(chunks)),
                [mpo_charge, masked, turned, kron] + chunks,
                [
                    pltpu.VMEM((2 * bond, *square), jnp.float32),
                    pltpu.VMEM((4 * bond, *square), jnp.float32),
                    pltpu.VMEM((pairs, *square), jnp.float32),
                ],
                limit=28,
            )
            kept.append(part)
            leaving = finished
        elif not last:
            own = call(
                functools.partial(own_kernel, spread, bond),
                shape_of(DOWN_VALUES, pairs, *square, dtype=jnp.float32),
                [VMEM] * 3,
                [masked, kron, finished],
                mixed_scratch,
            )
            shared = [mpo_charge, masked, turned, kron, own]
            scratch = mixed_scratch + [pltpu.VMEM((pairs, *square), jnp.float32)]
            outside = lax.ppermute(leaving, both, outer_halo)
            passed = []
            if spread > 1:
                inside = lax.ppermute(finished, both, inner_halo)
                passed.append(
                    call(
                        functools.partial(inner_kernel, chain_count, spread, bond),
                        full[0],
                        [SMEM] + [VMEM] * 5,
                        shared[:-1] + [finished, inside],
                        [
                            pltpu.VMEM((2 * bond, *square), jnp.float32),
                            pltpu.VMEM((4 * bond, *square), jnp.float32),
                            pltpu.VMEM((pairs, *square), jnp.float32),
                        ],
                        limit=28,
                    )
                    if site == 1
                    else call(
                        functools.partial(main_kernel, chain_count, spread, bond, False),
                        full[0],
                        [SMEM] + [VMEM] * 5,
                        shared + [inside],
                        scratch,
                        limit=28,
                    )
                )
            finished, part = call(
                functools.partial(main_kernel, chain_count, spread, bond, True),
                full,
                [SMEM] + [VMEM] * (5 + len(passed)),
                shared + [outside] + passed,
                scratch,
                limit=28,
            )
            leaving = passed[0] if spread == 2 else finished
            kept.append(part)
        else:
            parts = [
                call(
                    functools.partial(part_kernel, chain_count, spread, bond, ahead),
                    shape_of(keep, DOWN_VALUES, *square, dtype=dtype),
                    [SMEM] + [VMEM] * 4,
                    [mpo_charge, masked, entries, kron, finished],
                    mixed_scratch + [pltpu.VMEM((keep * PHYS, *square), jnp.float32)],
                    limit=28,
                )
                for ahead, entries, dtype in (
                    (1, more[0], jnp.bfloat16),
                    (0, turned, jnp.float32),
                )
            ]
            before = lax.ppermute(parts[0], both, halo)
            results = call(
                functools.partial(sort_kernel, chain_count, spread),
                [shape_of(local_bond, DOWN_VALUES, *square)] * (chain_count * spread),
                [VMEM] * (2 + len(kept)),
                [parts[1], before] + kept,
                [pltpu.VMEM((keep, DOWN_VALUES, *square), jnp.bfloat16)],
            )

    arrived = []
    for hop in range(chain_count):
        for turn in range(spread):
            piece = results[hop * spread + turn]
            if hop or turn:
                piece = lax.ppermute(
                    piece, both, [(flat(c, o), flat(c ^ hop, o ^ turn)) for c, o in everyone]
                )
            arrived.append(piece)
    return call(
        functools.partial(gather_kernel, chain_count, spread),
        shape_of(1, local_bond, sectors, *square),
        [VMEM] * len(arrived),
        arrived,
    )


def solution(mesh):
    return jax.shard_map(
        sweep,
        mesh=mesh,
        in_specs=(
            P("op", None, None, None),
            P("chain", None, None, None, None),
            P("chain", None, None, None, None),
            P("chain", None, None, None, None),
            P(),
            P(),
        ),
        out_specs=P("chain", "op", None, None, None),
        check_vma=False,
    )
```
